32 devices in a mesh: ex: 8 (over z, x), tp: 4 (over y, core).
Axes of the slice: x: 2, y: 2, z: 4, core: 2. Of those that a mesh axis runs over, the one named last changes fastest.
Arguments:
- acts: bfloat16 [8192, 4096], P('ex', 'tp'), may hold values from -6 to 6
- out_grads: bfloat16 [8192, 14336], P('ex', 'tp'), may hold values from -6 to 6
- basis_in: bfloat16 [4096, 128], P('tp'), may hold values from -0.09375 to 0.09375
- basis_out: bfloat16 [14336, 128], P('tp'), may hold values from -0.046875 to 0.046875
- eigen: float32 [128, 128], replicated, may hold values from 0.05 to 5
- query_grads: bfloat16 [256, 16384], P('ex'), may hold values from -0.046875 to 0.046875
- candidates: int32 [64, 4], P(('ex', 'tp')), may hold values from 0 to 7, as said below
- counts: int32 [64], P(('ex', 'tp')), may hold values from 2 to 4
- owner_map: int32 [8], replicated, may hold values from 0 to 7, each once
Outputs:
- scores: float32 [64, 4, 32], P(('ex', 'tp'))
The draws below stay inside these ranges and needn't reach their ends.
Inputs may be any that keep to these rules, and one draw needn't show every extreme that they name: `candidates`: each row holds 4 different query blocks; one block, the same for every row of a draw, is the first entry of every row; entries at or after counts[n] are not used.
All inputs are finite; a program needn't handle non-finite values.
Results may differ from the reference program's by a relative error of at most 0.0029.
Values may be sent and summed in bfloat16 or wider, within the bound.
A program may use at most 128 MiB of HBM per device.

```python
import math
import jax
import jax.numpy as jnp
from jax import lax

D = 4096
FF = 14336
KA = 128
KG = 128
SEQ = 128
QB = 32
C = 4
TOKENS = 8192
TRAIN = 64
KK = 16384
QUERIES = 256
N_EX = 8


def draw_candidates(key, part):
    key_noise = jax.random.fold_in(key, 11)
    key_pop = jax.random.fold_in(key, 12)
    key_hot = jax.random.fold_in(key, 13)
    noise = jax.random.randint(key_noise, (TRAIN, N_EX), 0, 1000)
    popular = jax.random.randint(key_pop, (N_EX,), 0, 4) * 500
    hot = jax.random.randint(key_hot, (), 0, N_EX)
    blocks = jnp.arange(N_EX, dtype=jnp.int32)
    score = noise + popular[None, :] + jnp.where(blocks == hot, 1000000, 0)[None, :]
    score = score * N_EX + blocks[None, :]
    values, picked = lax.top_k(score, C)
    return picked.astype(jnp.int32)


def draw_counts(key, part):
    key_len = jax.random.fold_in(key, 21)
    lengths = jax.random.randint(key_len, (TRAIN,), C // 2, C + 1)
    lengths = lengths.at[0].set(C)
    lengths = lengths.at[TRAIN - 1].set(C // 2)
    return lengths.astype(jnp.int32)


def levels(rng, extent, split, smallest, largest):
    def one(axis_at, blocks):
        draws = jax.random.uniform(jax.random.fold_in(jax.random.fold_in(rng, 6), axis_at), (blocks,), jnp.float32, smallest / len(split), largest / len(split))
        return jnp.repeat(jnp.exp(draws), extent[axis_at] // blocks).reshape((-1,) + (1,) * (len(extent) - axis_at - 1))

    loudness = one(*split[0])
    for cut in split[1:]:
        loudness = loudness * one(*cut)
    return loudness


def bell_draw(rng, extent, deviation, reach, shards=(), kind=jnp.bfloat16):
    gain = levels(rng, extent, shards, -0.22, 0.18) if shards else 1.0
    array = jax.random.normal(rng, extent, jnp.float32) * deviation * gain
    return jnp.minimum(jnp.maximum(array, -reach), reach).astype(kind)


def setup_inputs(seed: int = 0) -> dict:
    seeds = jax.random.split(jax.random.key(seed), 10)
    return {
        "acts": bell_draw(seeds[0], (TOKENS, D), 1.0, 6.0, ((0, 8), (1, 4))),
        "out_grads": bell_draw(seeds[1], (TOKENS, FF), 1.0, 6.0, ((0, 8), (1, 4))),
        "basis_in": bell_draw(seeds[2], (D, KA), D ** -0.5, 0.09375, ((0, 4),)),
        "basis_out": bell_draw(seeds[3], (FF, KG), FF ** -0.5, 0.046875, ((0, 4),)),
        "eigen": jnp.clip(jnp.exp(jax.random.uniform(seeds[4], (KG, KA), jnp.float32, math.log(0.05), math.log(5.0))), 0.05, 5.0),
        "query_grads": bell_draw(seeds[5], (QUERIES, KK), KK ** -0.5, 0.046875, ((0, 8),)),
        "candidates": draw_candidates(jax.random.fold_in(seeds[9], 71), 0),
        "counts": draw_counts(jax.random.fold_in(seeds[9], 71), 0),
        "owner_map": jax.random.permutation(seeds[8], N_EX).astype(jnp.int32),
    }


DAMP = 0.05


def reference(acts, out_grads, basis_in, basis_out, eigen, query_grads, candidates, counts, owner_map):
    proj_in = jnp.dot(acts, basis_in, preferred_element_type=jnp.float32)
    proj_out = jnp.dot(out_grads, basis_out, preferred_element_type=jnp.float32)
    seqs = proj_in.shape[0] // SEQ
    pin = proj_in.reshape(seqs, SEQ, KA)
    pout = proj_out.reshape(seqs, SEQ, KG)
    grad = jnp.einsum("nsg,nsa->nga", pout, pin, precision=lax.Precision.HIGHEST) / SEQ
    rows = (grad / (eigen + DAMP)).astype(jnp.bfloat16).reshape(seqs, KA * KG)
    blocks = query_grads.reshape(N_EX, QB, KA * KG)
    slots = jnp.arange(C, dtype=jnp.int32)

    def score_one(item):
        row, cand, count = item
        owners = owner_map[cand]
        chosen = blocks[owners].astype(jnp.float32)
        values = jnp.einsum("k,cqk->cq", row.astype(jnp.float32), chosen, precision=lax.Precision.HIGHEST)
        return jnp.where((slots < count)[:, None], values, jnp.float32(0.0))

    return lax.map(score_one, (rows, candidates, counts))
```

```python
import functools

import jax
import jax.numpy as jnp
from jax import lax
from jax.experimental import pallas as pl
from jax.experimental.pallas import tpu as pltpu
from jax.sharding import PartitionSpec as P

MESH = pl.DeviceIdType.MESH
KA = 128
KG = 128
SEQ = 128
DAMP = 0.05
TEAM = 4
SLICES = 4 * TEAM
DEPTH = KG // SLICES


def each(first, last, step):
    def body(i, carry):
        step(i)
        return carry

    lax.fori_loop(first, last, body, 0)


def kernel(
    owners,
    examples,
    acts_ref,
    grads_ref,
    bin_ref,
    bout_ref,
    eigen_ref,
    query_ref,
    cand_in,
    count_in,
    map_in,
    out_ref,
    acts_v,
    grads_v,
    bin_v,
    bout_v,
    eigen_v,
    query_v,
    part,
    landed,
    rows,
    gathered,
    wide,
    scores,
    returned,
    cand_ref,
    count_ref,
    map_ref,
    load_sem,
    piece_sem,
    tp_send,
    tp_recv,
    query_send,
    query_recv,
    row_send,
    row_recv,
    val_send,
    val_recv,
    team_ready,
    owner_ready,
):
    ex = lax.axis_index("ex")
    tp = lax.axis_index("tp")
    lo = ex % TEAM
    base = ex - lo
    me = lo * 4 + tp
    y, c = tp // 2, tp % 2
    near = 2 * y + (1 - c)
    far = 2 * (1 - y) + c
    tokens = examples * SEQ
    queries = query_ref.shape[0]
    width = query_ref.shape[1] // SLICES

    barrier = pltpu.get_barrier_semaphore()

    def greet(sem, e, t):
        pl.semaphore_signal(sem, inc=1, device_id=(e, t), device_id_type=MESH)

    def greet_team(sem):
        def step(e):
            for t in range(4):
                greet(sem, e, t)

        return step

    def await_ready(sem, count):
        @pl.when(count > 0)
        def _():
            pl.semaphore_wait(sem, count)

    for j in range(1, 4):
        greet(barrier, ex, (tp + j) % 4)
    each(ex + 1, base + TEAM, greet_team(barrier))
    each(base + TEAM, owners, lambda e: greet(barrier, e, tp))

    chunks = (2 * (1 - y) + (1 - c), far, near, tp)

    def load(src, dst, sem):
        return pltpu.make_async_copy(src, dst, load_sem.at[sem])

    load_b = (load(bin_ref, bin_v, 0), load(bout_ref, bout_v, 1))
    load_e = load(eigen_ref, eigen_v, 2)
    mine = query_ref.at[:, pl.ds(pl.multiple_of(me * width, width), width)]
    own_rows = pl.ds(pl.multiple_of(ex * queries, queries), queries)
    load_q = load(mine, query_v.at[own_rows], 3)
    tables = (
        load(cand_in, cand_ref, 4),
        load(count_in, count_ref, 5),
        load(map_in, map_ref, 6),
    )
    pieces = {}
    for i, d in enumerate(chunks):
        for n in range(examples):
            here = pl.ds(pl.multiple_of(d * tokens + n * SEQ, SEQ), SEQ)
            there = pl.ds(n * SEQ, SEQ)
            at = 2 * (i * examples + n)
            pieces[i, n] = (
                pltpu.make_async_copy(
                    acts_ref.at[here], acts_v.at[i, there], piece_sem.at[at]
                ),
                pltpu.make_async_copy(
                    grads_ref.at[here], grads_v.at[i, there], piece_sem.at[at + 1]
                ),
            )
    order = [(i, n) for n in range(examples) for i in (0, 1)]
    order += [(i, n) for i in (2, 3) for n in range(examples)]
    for copy in load_b:
        copy.start()
    for key in order:
        for copy in pieces[key]:
            copy.start()
    for copy in (load_e, load_q, *tables):
        copy.start()

    pl.semaphore_wait(barrier, 3 + 4 * lo + base)
    each(base, ex, greet_team(team_ready))
    each(0, base, lambda e: greet(owner_ready, e, tp))

    def pass_query(e):
        k = (e % TEAM) * 4 + tp
        return pltpu.make_async_remote_copy(
            src_ref=query_ref.at[:, pl.ds(pl.multiple_of(k * width, width), width)],
            dst_ref=query_v.at[own_rows],
            send_sem=query_send.at[e],
            recv_sem=query_recv.at[ex],
            device_id=(e, tp),
            device_id_type=MESH,
        )

    def take_query(e):
        return pltpu.make_async_remote_copy(
            src_ref=mine,
            dst_ref=query_v.at[pl.ds(pl.multiple_of(e * queries, queries), queries)],
            send_sem=query_send.at[e],
            recv_sem=query_recv.at[e],
            device_id=(e, tp),
            device_id_type=MESH,
        )

    def others(step):
        each(0, ex, step)
        each(ex + 1, owners, step)

    each(0, ex, lambda e: pass_query(e).start())
    for copy in load_b:
        copy.wait()

    def project(i, n):
        for copy in pieces[i, n]:
            copy.wait()
        span = pl.ds(n * SEQ, SEQ)
        part[i, span, :KA] = jnp.dot(
            acts_v[i, span], bin_v[...], preferred_element_type=jnp.float32
        )
        part[i, span, KA:] = jnp.dot(
            grads_v[i, span], bout_v[...], preferred_element_type=jnp.float32
        )

    def send(i, slot, n, peer):
        sem = slot * examples + n
        copy = pltpu.make_async_remote_copy(
            src_ref=part.at[i, pl.ds(n * SEQ, SEQ)],
            dst_ref=landed.at[slot, pl.ds(n * SEQ, SEQ)],
            send_sem=tp_send.at[sem],
            recv_sem=tp_recv.at[sem],
            device_id=(ex, peer),
            device_id_type=MESH,
        )
        copy.start()
        return copy

    first, across, second = [], [], []
    for n in range(examples):
        project(0, n)
        first.append(send(0, 0, n, near))
        project(1, n)
    for n in range(examples):
        first[n].wait_recv()
        span = slice(n * SEQ, (n + 1) * SEQ)
        part[1, span] += landed[0, span]
        across.append(send(1, 1, n, far))
    for n in range(examples):
        project(2, n)
        second.append(send(2, 2, n, near))
    for n in range(examples):
        project(3, n)
    load_e.wait()
    scale = (eigen_v[...] + DAMP) * SEQ
    await_ready(team_ready, 4 * (base + TEAM - 1 - ex))
    each(ex + 1, base + TEAM, lambda e: pass_query(e).start())
    await_ready(owner_ready, owners - TEAM - base)
    each(base + TEAM, owners, lambda e: pass_query(e).start())

    ratios = []
    for n in range(examples):
        span = slice(n * SEQ, (n + 1) * SEQ)
        second[n].wait_recv()
        both = part[3, span] + landed[2, span]
        across[n].wait_recv()
        both = both + landed[1, span]
        grad = lax.dot_general(
            both[:, KA:],
            both[:, :KA],
            (((0,), (0,)), ((), ())),
            precision=lax.Precision.HIGHEST,
            preferred_element_type=jnp.float32,
        )
        ratios.append((grad / scale).reshape(SLICES, DEPTH, KA))
    rows[...] = jnp.concatenate(ratios, axis=1).astype(jnp.bfloat16)

    offsets = [(i, j) for i in range(TEAM) for j in range(4)][1:]
    row_copies = []
    for i, j in reversed(offsets):
        e, t = (lo + i) % TEAM, (tp + j) % 4
        k = e * 4 + t
        copy = pltpu.make_async_remote_copy(
            src_ref=rows.at[k],
            dst_ref=gathered.at[me],
            send_sem=row_send.at[k],
            recv_sem=row_recv.at[me],
            device_id=(base + e, t),
            device_id_type=MESH,
        )
        copy.start()
        row_copies.append(copy)
    gathered[me] = rows[me]
    for copy in tables:
        copy.wait()
    slot_total = cand_ref.shape[1]
    line = lax.broadcasted_iota(jnp.int32, (examples * slot_total, 1), 0)
    codes = jnp.full((examples * slot_total, 1), -1, jnp.int32)
    for n in range(examples):
        for s in range(slot_total):
            code = jnp.where(s < count_ref[n], map_ref[cand_ref[n, s]], -1)
            codes = jnp.where(line == n * slot_total + s, code, codes)
    load_q.wait()
    others(lambda e: take_query(e).wait_recv())

    def arrived(src_buf, dst_buf, send_sem, recv_sem, k):
        return pltpu.make_async_remote_copy(
            src_ref=src_buf.at[k],
            dst_ref=dst_buf.at[k],
            send_sem=send_sem.at[k],
            recv_sem=recv_sem.at[k],
            device_id=(base + k // 4, k % 4),
            device_id_type=MESH,
        )

    peers = [((lo + i) % TEAM) * 4 + (tp + j) % 4 for i, j in offsets]
    for k in peers:
        arrived(rows, gathered, row_send, row_recv, k).wait_recv()
    wide[...] = gathered[...].astype(jnp.float32).reshape(SLICES * examples * DEPTH, KA)
    lines = jnp.concatenate(
        [wide[pl.ds(g, SLICES * examples, stride=DEPTH), :] for g in range(DEPTH)], axis=1
    ).astype(jnp.bfloat16)
    values = lax.dot_general(
        lines,
        query_v[...],
        (((1,), (1,)), ((), ())),
        preferred_element_type=jnp.float32,
    )
    for k in range(SLICES):
        scores[k] = values[k * examples : (k + 1) * examples, :]
    val_copies = []
    for i, j in reversed(offsets):
        e, t = (lo + i) % TEAM, (tp + j) % 4
        k = e * 4 + t
        copy = pltpu.make_async_remote_copy(
            src_ref=scores.at[k],
            dst_ref=returned.at[me],
            send_sem=val_send.at[k],
            recv_sem=val_recv.at[me],
            device_id=(base + e, t),
            device_id_type=MESH,
        )
        copy.start()
        val_copies.append(copy)
    returned[me] = scores[me]
    for copy in (*first, *across, *second, *row_copies):
        copy.wait_send()
    others(lambda e: pass_query(e).wait_send())
    for k in peers:
        arrived(scores, returned, val_send, val_recv, k).wait_recv()
    sums = jnp.sum(returned[...], axis=0)
    total = sums.shape[1]
    block = lax.broadcasted_iota(jnp.int32, (1, total), 1) // queries
    spread = jnp.concatenate(
        [jnp.broadcast_to(sums[n : n + 1], (slot_total, total)) for n in range(examples)], axis=0
    )
    kept = jnp.where(block == codes, spread, 0.0)
    lanes = sum(kept[:, a : a + 128] for a in range(0, total, 128))
    chosen = sum(lanes[:, a : a + queries] for a in range(0, 128, queries))
    for n in range(examples):
        out_ref[n] = chosen[n * slot_total : (n + 1) * slot_total]
    for copy in val_copies:
        copy.wait_send()


def shards(acts, out_grads, basis_in, basis_out, eigen, query_grads, candidates, counts, owner_map):
    owners = lax.axis_size("ex")
    assert lax.axis_size("tp") == 4 and owners % TEAM == 0
    examples, slot_total = candidates.shape
    tokens = examples * SEQ
    queries = query_grads.shape[0]
    width = query_grads.shape[1] // SLICES
    assert query_grads.shape[1] == KA * KG and 128 % queries == 0
    vmem = pltpu.VMEM
    dma = pltpu.SemaphoreType.DMA
    return pl.pallas_call(
        functools.partial(kernel, owners, examples),
        out_shape=jax.ShapeDtypeStruct((examples, slot_total, queries), jnp.float32),
        in_specs=[pl.BlockSpec(memory_space=pl.ANY)] * 9,
        out_specs=pl.BlockSpec(memory_space=pltpu.VMEM),
        scratch_shapes=[
            vmem((4, tokens, acts.shape[1]), jnp.bfloat16),
            vmem((4, tokens, out_grads.shape[1]), jnp.bfloat16),
            vmem(basis_in.shape, jnp.bfloat16),
            vmem(basis_out.shape, jnp.bfloat16),
            vmem(eigen.shape, jnp.float32),
            vmem((owners * queries, width), jnp.bfloat16),
            vmem((4, tokens, KA + KG), jnp.float32),
            vmem((3, tokens, KA + KG), jnp.float32),
            vmem((SLICES, examples * DEPTH, KA), jnp.bfloat16),
            vmem((SLICES, examples * DEPTH, KA), jnp.bfloat16),
            vmem((SLICES * examples * DEPTH, KA), jnp.float32),
            vmem((SLICES, examples, owners * queries), jnp.float32),
            vmem((SLICES, examples, owners * queries), jnp.float32),
            pltpu.SMEM(candidates.shape, jnp.int32),
            pltpu.SMEM(counts.shape, jnp.int32),
            pltpu.SMEM(owner_map.shape, jnp.int32),
            dma((7,)),
            dma((8 * examples,)),
            dma((3 * examples,)),
            dma((3 * examples,)),
            dma((owners,)),
            dma((owners,)),
            dma((SLICES,)),
            dma((SLICES,)),
            dma((SLICES,)),
            dma((SLICES,)),
            pltpu.SemaphoreType.REGULAR,
            pltpu.SemaphoreType.REGULAR,
        ],
        compiler_params=pltpu.CompilerParams(
            collective_id=0, has_side_effects=True, vmem_limit_bytes=60 << 20
        ),
    )(acts, out_grads, basis_in, basis_out, eigen, query_grads, candidates, counts, owner_map)


def solution(mesh):
    in_specs = (
        P("ex", "tp"),
        P("ex", "tp"),
        P("tp", None),
        P("tp", None),
        P(),
        P("ex", None),
        P(("ex", "tp"), None),
        P(("ex", "tp")),
        P(),
    )
    out_specs = P(("ex", "tp"), None, None)
    return jax.shard_map(shards, mesh=mesh, in_specs=in_specs, out_specs=out_specs, check_vma=False)
```

```python
import functools

import jax
import jax.numpy as jnp
from jax import lax
from jax.experimental import pallas as pl
from jax.experimental.pallas import tpu as pltpu
from jax.sharding import PartitionSpec as P

MESH = pl.DeviceIdType.MESH
KA = 128
KG = 128
SEQ = 128
DAMP = 0.05
TEAM = 4
SLICES = 4 * TEAM
DEPTH = KG // SLICES
LEVELS = 32767.0
TINY = 1e-30


def each(first, last, step):
    def body(i, carry):
        step(i)
        return carry

    lax.fori_loop(first, last, body, 0)


def kernel(
    owners,
    examples,
    acts_ref,
    grads_ref,
    bin_ref,
    bout_ref,
    eigen_ref,
    query_ref,
    cand_in,
    count_in,
    map_in,
    out_ref,
    acts_v,
    grads_v,
    bin_v,
    bout_v,
    eigen_v,
    query_v,
    staged,
    part,
    landed,
    coded,
    steps,
    landed_coded,
    landed_steps,
    rows,
    gathered,
    wide,
    scores,
    returned,
    cand_ref,
    count_ref,
    map_ref,
    load_sem,
    piece_sem,
    tp_send,
    tp_recv,
    query_send,
    query_recv,
    row_send,
    row_recv,
    val_send,
    val_recv,
    tp_ready,
    ready,
    team_ready,
):
    ex = lax.axis_index("ex")
    tp = lax.axis_index("tp")
    lo = ex % TEAM
    base = ex - lo
    me = lo * 4 + tp
    y, c = tp // 2, tp % 2
    near = 2 * y + (1 - c)
    far = 2 * (1 - y) + c
    tokens = examples * SEQ
    queries = query_ref.shape[0]
    width = query_ref.shape[1] // SLICES

    barrier = pltpu.get_barrier_semaphore()

    def greet(sem, e, t):
        pl.semaphore_signal(sem, inc=1, device_id=(e, t), device_id_type=MESH)

    def await_all(sem, count):
        @pl.when(count > 0)
        def _():
            pl.semaphore_wait(sem, count)

    def greet_team(sem):
        def step(e):
            for t in range(4):
                greet(sem, e, t)

        return step

    def when(condition, step):
        @pl.when(condition)
        def _():
            step()

    when(c == 0, lambda: greet(barrier, ex, near))
    when(y == 0, lambda: greet(barrier, ex, far))

    chunks = (2 * (1 - y) + (1 - c), far, near, tp)

    def load(src, dst, sem):
        return pltpu.make_async_copy(src, dst, load_sem.at[sem])

    load_b = (load(bin_ref, bin_v, 0), load(bout_ref, bout_v, 1))
    load_e = load(eigen_ref, eigen_v, 2)
    own_rows = pl.ds(pl.multiple_of(ex * queries, queries), queries)

    def slice_of(l):
        return query_ref.at[:, pl.ds(pl.multiple_of((l * 4 + tp) * width, width), width)]

    load_q = load(slice_of(lo), query_v.at[own_rows], 3)
    load_s = [load(slice_of(l), staged.at[l], 7 + l) for l in range(TEAM)]
    tables = (
        load(cand_in, cand_ref, 4),
        load(count_in, count_ref, 5),
        load(map_in, map_ref, 6),
    )
    pieces = {}
    for i, d in enumerate(chunks):
        for n in range(examples):
            here = pl.ds(pl.multiple_of(d * tokens + n * SEQ, SEQ), SEQ)
            there = pl.ds(n * SEQ, SEQ)
            at = 2 * (i * examples + n)
            pieces[i, n] = (
                pltpu.make_async_copy(
                    acts_ref.at[here], acts_v.at[i, there], piece_sem.at[at]
                ),
                pltpu.make_async_copy(
                    grads_ref.at[here], grads_v.at[i, there], piece_sem.at[at + 1]
                ),
            )
    order = [(i, n) for n in range(examples) for i in (0, 1)]
    order += [(i, n) for i in (2, 3) for n in range(examples)]
    for copy in (*load_s, *load_b):
        copy.start()
    for key in order:
        for copy in pieces[key]:
            copy.start()
    for copy in (load_e, load_q, *tables):
        copy.start()

    each(ex + 1, base + TEAM, greet_team(barrier))
    each(base + TEAM, owners, lambda e: greet(barrier, e, tp))
    await_all(barrier, c + y + 4 * lo + base)
    when(c == 1, lambda: greet(tp_ready.at[0], ex, near))
    when(y == 1, lambda: greet(tp_ready.at[1], ex, far))
    each(0, ex, lambda e: greet(ready.at[ex], e, tp))

    def pass_query(e):
        return pltpu.make_async_remote_copy(
            src_ref=staged.at[e % TEAM],
            dst_ref=query_v.at[own_rows],
            send_sem=query_send.at[e],
            recv_sem=query_recv.at[ex],
            device_id=(e, tp),
            device_id_type=MESH,
        )

    def take_query(e):
        return pltpu.make_async_remote_copy(
            src_ref=staged.at[e % TEAM],
            dst_ref=query_v.at[pl.ds(pl.multiple_of(e * queries, queries), queries)],
            send_sem=query_send.at[e],
            recv_sem=query_recv.at[e],
            device_id=(e, tp),
            device_id_type=MESH,
        )

    def others(step):
        each(0, ex, step)
        each(ex + 1, owners, step)

    for copy in load_s:
        copy.wait()
    each(0, ex, lambda e: pass_query(e).start())
    for copy in load_b:
        copy.wait()

    def project(i, n):
        for copy in pieces[i, n]:
            copy.wait()
        span = pl.ds(n * SEQ, SEQ)
        part[i, span, :KA] = jnp.dot(
            acts_v[i, span], bin_v[...], preferred_element_type=jnp.float32
        )
        part[i, span, KA:] = jnp.dot(
            grads_v[i, span], bout_v[...], preferred_element_type=jnp.float32
        )

    def send(src, dst, sem, peer):
        copy = pltpu.make_async_remote_copy(
            src_ref=src,
            dst_ref=dst,
            send_sem=tp_send.at[sem],
            recv_sem=tp_recv.at[sem],
            device_id=(ex, peer),
            device_id_type=MESH,
        )
        copy.start()
        return copy

    def pass_up(e):
        pl.semaphore_wait(ready.at[e], 1)
        pass_query(e).start()

    first, across, second = [], [], []

    def send_near(i, slot, n):
        span = pl.ds(n * SEQ, SEQ)
        return send(part.at[i, span], landed.at[slot, span], slot * examples + n, near)

    def forward(n):
        first[n].wait_recv()
        span = slice(n * SEQ, (n + 1) * SEQ)
        both = part[1, span] + landed[0, span]
        top = jnp.maximum(jnp.max(jnp.abs(both), axis=0, keepdims=True), TINY)
        steps[n] = top * (1.0 / LEVELS)
        coded[n] = jnp.round(both * (LEVELS / top)).astype(jnp.int32).astype(jnp.int16)
        if n == 0:
            when(y == 0, lambda: pl.semaphore_wait(tp_ready.at[1], 1))
        sem = 2 * examples + 2 * n
        across.append(
            (
                send(coded.at[n], landed_coded.at[n], sem, far),
                send(steps.at[n], landed_steps.at[n], sem + 1, far),
            )
        )

    for n in range(examples):
        project(0, n)
        if n == 0:
            when(c == 0, lambda: pl.semaphore_wait(tp_ready.at[0], 1))
        first.append(send_near(0, 0, n))
        if n > 0:
            forward(n - 1)
        project(1, n)
    forward(examples - 1)
    each(base, ex, greet_team(team_ready))
    each(ex + 1, base + TEAM, pass_up)
    for n in range(examples):
        project(2, n)
        second.append(send_near(2, 1, n))
    for n in range(examples):
        project(3, n)
    load_e.wait()
    scale = (eigen_v[...] + DAMP) * SEQ
    each(base + TEAM, owners, pass_up)
    await_all(team_ready, 4 * (base + TEAM - 1 - ex))

    ratios = []
    for n in range(examples):
        span = slice(n * SEQ, (n + 1) * SEQ)
        second[n].wait_recv()
        both = part[3, span] + landed[1, span]
        for copy in across[n]:
            copy.wait_recv()
        both += landed_coded[n].astype(jnp.int32).astype(jnp.float32) * landed_steps[n]
        grad = lax.dot_general(
            both[:, KA:],
            both[:, :KA],
            (((0,), (0,)), ((), ())),
            precision=lax.Precision.HIGHEST,
            preferred_element_type=jnp.float32,
        )
        ratios.append((grad / scale).reshape(SLICES, DEPTH, KA))
    rows[...] = jnp.concatenate(ratios, axis=1).astype(jnp.bfloat16)

    offsets = [(i, j) for i in range(TEAM) for j in range(4)][1:]
    row_copies = []
    for i, j in reversed(offsets):
        e, t = (lo + i) % TEAM, (tp + j) % 4
        k = e * 4 + t
        copy = pltpu.make_async_remote_copy(
            src_ref=rows.at[k],
            dst_ref=gathered.at[me],
            send_sem=row_send.at[k],
            recv_sem=row_recv.at[me],
            device_id=(base + e, t),
            device_id_type=MESH,
        )
        copy.start()
        row_copies.append(copy)
    gathered[me] = rows[me]
    for copy in tables:
        copy.wait()
    slot_total = cand_ref.shape[1]
    line = lax.broadcasted_iota(jnp.int32, (examples * slot_total, 1), 0)
    codes = jnp.full((examples * slot_total, 1), -1, jnp.int32)
    for n in range(examples):
        for s in range(slot_total):
            code = jnp.where(s < count_ref[n], map_ref[cand_ref[n, s]], -1)
            codes = jnp.where(line == n * slot_total + s, code, codes)
    load_q.wait()
    others(lambda e: take_query(e).wait_recv())

    def arrived(src_buf, dst_buf, send_sem, recv_sem, k):
        return pltpu.make_async_remote_copy(
            src_ref=src_buf.at[k],
            dst_ref=dst_buf.at[k],
            send_sem=send_sem.at[k],
            recv_sem=recv_sem.at[k],
            device_id=(base + k // 4, k % 4),
            device_id_type=MESH,
        )

    peers = [((lo + i) % TEAM) * 4 + (tp + j) % 4 for i, j in offsets]
    for k in peers:
        arrived(rows, gathered, row_send, row_recv, k).wait_recv()
    wide[...] = gathered[...].astype(jnp.float32).reshape(SLICES * examples * DEPTH, KA)
    lines = jnp.concatenate(
        [wide[pl.ds(g, SLICES * examples, stride=DEPTH), :] for g in range(DEPTH)], axis=1
    ).astype(jnp.bfloat16)
    values = lax.dot_general(
        lines,
        query_v[...],
        (((1,), (1,)), ((), ())),
        preferred_element_type=jnp.float32,
    )
    for k in range(SLICES):
        scores[k] = values[k * examples : (k + 1) * examples, :]
    val_copies = []
    for i, j in reversed(offsets):
        e, t = (lo + i) % TEAM, (tp + j) % 4
        k = e * 4 + t
        copy = pltpu.make_async_remote_copy(
            src_ref=scores.at[k],
            dst_ref=returned.at[me],
            send_sem=val_send.at[k],
            recv_sem=val_recv.at[me],
            device_id=(base + e, t),
            device_id_type=MESH,
        )
        copy.start()
        val_copies.append(copy)
    returned[me] = scores[me]
    for copy in (*first, *sum(across, ()), *second, *row_copies):
        copy.wait_send()
    others(lambda e: pass_query(e).wait_send())
    for k in peers:
        arrived(scores, returned, val_send, val_recv, k).wait_recv()
    sums = jnp.sum(returned[...], axis=0)
    total = sums.shape[1]
    block = lax.broadcasted_iota(jnp.int32, (1, total), 1) // queries
    spread = jnp.concatenate(
        [jnp.broadcast_to(sums[n : n + 1], (slot_total, total)) for n in range(examples)], axis=0
    )
    kept = jnp.where(block == codes, spread, 0.0)
    lanes = sum(kept[:, a : a + 128] for a in range(0, total, 128))
    chosen = sum(lanes[:, a : a + queries] for a in range(0, 128, queries))
    for n in range(examples):
        out_ref[n] = chosen[n * slot_total : (n + 1) * slot_total]
    for copy in val_copies:
        copy.wait_send()


def shards(acts, out_grads, basis_in, basis_out, eigen, query_grads, candidates, counts, owner_map):
    owners = lax.axis_size("ex")
    assert lax.axis_size("tp") == 4 and owners % TEAM == 0
    examples, slot_total = candidates.shape
    tokens = examples * SEQ
    queries = query_grads.shape[0]
    width = query_grads.shape[1] // SLICES
    assert query_grads.shape[1] == KA * KG and 128 % queries == 0
    vmem = pltpu.VMEM
    dma = pltpu.SemaphoreType.DMA
    return pl.pallas_call(
        functools.partial(kernel, owners, examples),
        out_shape=jax.ShapeDtypeStruct((examples, slot_total, queries), jnp.float32),
        in_specs=[pl.BlockSpec(memory_space=pl.ANY)] * 9,
        out_specs=pl.BlockSpec(memory_space=pltpu.VMEM),
        scratch_shapes=[
            vmem((4, tokens, acts.shape[1]), jnp.bfloat16),
            vmem((4, tokens, out_grads.shape[1]), jnp.bfloat16),
            vmem(basis_in.shape, jnp.bfloat16),
            vmem(basis_out.shape, jnp.bfloat16),
            vmem(eigen.shape, jnp.float32),
            vmem((owners * queries, width), jnp.bfloat16),
            vmem((TEAM, queries, width), jnp.bfloat16),
            vmem((4, tokens, KA + KG), jnp.float32),
            vmem((2, tokens, KA + KG), jnp.float32),
            vmem((examples, SEQ, KA + KG), jnp.int16),
            vmem((examples, 1, KA + KG), jnp.float32),
            vmem((examples, SEQ, KA + KG), jnp.int16),
            vmem((examples, 1, KA + KG), jnp.float32),
            vmem((SLICES, examples * DEPTH, KA), jnp.bfloat16),
            vmem((SLICES, examples * DEPTH, KA), jnp.bfloat16),
            vmem((SLICES * examples * DEPTH, KA), jnp.float32),
            vmem((SLICES, examples, owners * queries), jnp.float32),
            vmem((SLICES, examples, owners * queries), jnp.float32),
            pltpu.SMEM(candidates.shape, jnp.int32),
            pltpu.SMEM(counts.shape, jnp.int32),
            pltpu.SMEM(owner_map.shape, jnp.int32),
            dma((7 + TEAM,)),
            dma((8 * examples,)),
            dma((4 * examples,)),
            dma((4 * examples,)),
            dma((owners,)),
            dma((owners,)),
            dma((SLICES,)),
            dma((SLICES,)),
            dma((SLICES,)),
            dma((SLICES,)),
            pltpu.SemaphoreType.REGULAR((2,)),
            pltpu.SemaphoreType.REGULAR((owners,)),
            pltpu.SemaphoreType.REGULAR,
        ],
        compiler_params=pltpu.CompilerParams(
            collective_id=0, has_side_effects=True, vmem_limit_bytes=60 << 20
        ),
    )(acts, out_grads, basis_in, basis_out, eigen, query_grads, candidates, counts, owner_map)


def solution(mesh):
    in_specs = (
        P("ex", "tp"),
        P("ex", "tp"),
        P("tp", None),
        P("tp", None),
        P(),
        P("ex", None),
        P(("ex", "tp"), None),
        P(("ex", "tp")),
        P(),
    )
    out_specs = P(("ex", "tp"), None, None)
    return jax.shard_map(shards, mesh=mesh, in_specs=in_specs, out_specs=out_specs, check_vma=False)
```

```python
import functools

import jax
import jax.numpy as jnp
from jax import lax
from jax.experimental import pallas as pl
from jax.experimental.pallas import tpu as pltpu
from jax.sharding import PartitionSpec as P

MESH = pl.DeviceIdType.MESH
KA = 128
KG = 128
SEQ = 128
DAMP = 0.05
DISTRICT = 8
FIRST = 2
TEAM = 4
SLICES = 4 * TEAM
SOURCES = 4 * DISTRICT
BATCHES = 2
SHARE = SOURCES // BATCHES
DEPTH = KG // SLICES
PAIR = 2
LEVELS = 32767.0
TINY = 1e-30


def each(first, last, step):
    def body(i, carry):
        step(i)
        return carry

    lax.fori_loop(first, last, body, 0)


def kernel(
    owners,
    examples,
    acts_ref,
    grads_ref,
    bin_ref,
    bout_ref,
    eigen_ref,
    query_ref,
    cand_in,
    count_in,
    map_in,
    out_ref,
    acts_v,
    grads_v,
    bin_v,
    bout_v,
    eigen_v,
    query_v,
    staged,
    part,
    landed,
    coded,
    steps,
    landed_coded,
    landed_steps,
    rows,
    gathered,
    wide,
    scores,
    returned,
    cand_ref,
    count_ref,
    map_ref,
    load_sem,
    piece_sem,
    tp_send,
    tp_recv,
    query_send,
    query_recv,
    row_send,
    row_recv,
    val_send,
    val_recv,
    tp_ready,
    ready,
    team_ready,
):
    ex = lax.axis_index("ex")
    tp = lax.axis_index("tp")
    place = ex % DISTRICT
    home = ex - place
    spot = place * 4 + tp
    centre = (place >= FIRST) & (place < FIRST + TEAM)
    me = jnp.where(centre, (place - FIRST) * 4 + tp, 0)
    y, c = tp // 2, tp % 2
    near = 2 * y + (1 - c)
    far = 2 * (1 - y) + c
    tokens = examples * SEQ
    queries = query_ref.shape[0]
    width = query_ref.shape[1] // SLICES

    barrier = pltpu.get_barrier_semaphore()

    def greet(sem, e, t):
        pl.semaphore_signal(sem, inc=1, device_id=(e, t), device_id_type=MESH)

    def await_all(sem, count):
        @pl.when(count > 0)
        def _():
            pl.semaphore_wait(sem, count)

    def is_centre(e):
        at = e % DISTRICT
        return (at >= FIRST) & (at < FIRST + TEAM)

    def linked(first, last, step):
        def visit(e):
            pl.when(centre | is_centre(e))(lambda: step(e))

        each(first, last, visit)

    def number(first, last):
        def count(e, sofar):
            return sofar + (centre | is_centre(e)).astype(jnp.int32)

        return lax.fori_loop(first, last, count, 0)

    def greet_all(sem):
        def step(e):
            for t in range(4):
                greet(sem, e, t)

        return step

    def when(condition, step):
        @pl.when(condition)
        def _():
            step()

    when(c == 0, lambda: greet(barrier, ex, near))
    when(y == 0, lambda: greet(barrier, ex, far))

    chunks = (2 * (1 - y) + (1 - c), far, near, tp)

    def load(src, dst, sem):
        return pltpu.make_async_copy(src, dst, load_sem.at[sem])

    load_b = (load(bin_ref, bin_v, 0), load(bout_ref, bout_v, 1))
    load_e = load(eigen_ref, eigen_v, 2)
    own_rows = pl.ds(pl.multiple_of(ex * queries, queries), queries)

    def slice_of(l):
        return query_ref.at[:, pl.ds(pl.multiple_of((l * 4 + tp) * width, width), width)]

    load_q = load(slice_of(jnp.where(centre, place - FIRST, 0)), query_v.at[own_rows], 3)
    load_s = [load(slice_of(l), staged.at[l], 7 + l) for l in range(TEAM)]
    tables = (
        load(cand_in, cand_ref, 4),
        load(count_in, count_ref, 5),
        load(map_in, map_ref, 6),
    )
    pieces = {}
    for i, d in enumerate(chunks):
        for n in range(examples):
            here = pl.ds(pl.multiple_of(d * tokens + n * SEQ, SEQ), SEQ)
            there = pl.ds(n * SEQ, SEQ)
            at = 2 * (i * examples + n)
            pieces[i, n] = (
                pltpu.make_async_copy(
                    acts_ref.at[here], acts_v.at[i, there], piece_sem.at[at]
                ),
                pltpu.make_async_copy(
                    grads_ref.at[here], grads_v.at[i, there], piece_sem.at[at + 1]
                ),
            )
    order = [(i, n) for n in range(examples) for i in (0, 1)]
    order += [(i, n) for i in (2, 3) for n in range(examples)]
    for copy in (*load_s, *load_b):
        copy.start()
    for key in order:
        for copy in pieces[key]:
            copy.start()
    for copy in (load_e, load_q, *tables):
        copy.start()

    linked(ex + 1, home + DISTRICT, greet_all(barrier))
    linked(home + DISTRICT, owners, lambda e: greet(barrier, e, tp))
    await_all(barrier, c + y + 4 * number(home, ex) + number(0, home))
    when(c == 1, lambda: greet(tp_ready.at[0], ex, near))
    when(y == 1, lambda: greet(tp_ready.at[1], ex, far))
    when(centre, lambda: each(0, ex, lambda e: greet(ready.at[ex], e, tp)))

    def pass_query(e):
        return pltpu.make_async_remote_copy(
            src_ref=staged.at[e % DISTRICT - FIRST],
            dst_ref=query_v.at[own_rows],
            send_sem=query_send.at[e],
            recv_sem=query_recv.at[ex],
            device_id=(e, tp),
            device_id_type=MESH,
        )

    def take_query(e):
        return pltpu.make_async_remote_copy(
            src_ref=staged.at[0],
            dst_ref=query_v.at[pl.ds(pl.multiple_of(e * queries, queries), queries)],
            send_sem=query_send.at[e],
            recv_sem=query_recv.at[e],
            device_id=(e, tp),
            device_id_type=MESH,
        )

    def to_centres(first, last, step):
        def visit(e):
            pl.when(is_centre(e))(lambda: step(e))

        each(first, last, visit)

    def others(visit, step):
        visit(0, ex, step)
        visit(ex + 1, owners, step)

    for copy in load_s:
        copy.wait()
    to_centres(0, ex, lambda e: pass_query(e).start())
    for copy in load_b:
        copy.wait()

    def project(i, n):
        for copy in pieces[i, n]:
            copy.wait()
        span = pl.ds(n * SEQ, SEQ)
        part[i, span, :KA] = jnp.dot(
            acts_v[i, span], bin_v[...], preferred_element_type=jnp.float32
        )
        part[i, span, KA:] = jnp.dot(
            grads_v[i, span], bout_v[...], preferred_element_type=jnp.float32
        )

    def send(src, dst, sem, peer):
        copy = pltpu.make_async_remote_copy(
            src_ref=src,
            dst_ref=dst,
            send_sem=tp_send.at[sem],
            recv_sem=tp_recv.at[sem],
            device_id=(ex, peer),
            device_id_type=MESH,
        )
        copy.start()
        return copy

    def pass_up(e):
        pl.semaphore_wait(ready.at[e], 1)
        pass_query(e).start()

    soon = jnp.minimum((ex // PAIR + 2) * PAIR, owners)
    first, across, second = [], [], []

    def send_near(i, slot, n):
        span = pl.ds(n * SEQ, SEQ)
        return send(part.at[i, span], landed.at[slot, span], slot * examples + n, near)

    def forward(n):
        first[n].wait_recv()
        span = slice(n * SEQ, (n + 1) * SEQ)
        both = part[1, span] + landed[0, span]
        top = jnp.maximum(jnp.max(jnp.abs(both), axis=0, keepdims=True), TINY)
        steps[n] = top * (1.0 / LEVELS)
        coded[n] = jnp.round(both * (LEVELS / top)).astype(jnp.int32).astype(jnp.int16)
        if n == 0:
            when(y == 0, lambda: pl.semaphore_wait(tp_ready.at[1], 1))
        sem = 2 * examples + 2 * n
        across.append(
            (
                send(coded.at[n], landed_coded.at[n], sem, far),
                send(steps.at[n], landed_steps.at[n], sem + 1, far),
            )
        )

    for n in range(examples):
        project(0, n)
        if n == 0:
            when(c == 0, lambda: pl.semaphore_wait(tp_ready.at[0], 1))
        first.append(send_near(0, 0, n))
        if n > 0:
            forward(n - 1)
        project(1, n)
        if n == 0:
            to_centres(ex + 1, soon, pass_up)
    forward(examples - 1)
    to_centres(soon, owners, pass_up)
    linked(home, ex, greet_all(team_ready))
    for n in range(examples):
        project(2, n)
        second.append(send_near(2, 1, n))
    for n in range(examples):
        project(3, n)
    load_e.wait()
    scale = (eigen_v[...] + DAMP) * SEQ
    await_all(team_ready, 4 * number(ex + 1, home + DISTRICT))

    ratios = []
    for n in range(examples):
        span = slice(n * SEQ, (n + 1) * SEQ)
        second[n].wait_recv()
        both = part[3, span] + landed[1, span]
        for copy in across[n]:
            copy.wait_recv()
        both += landed_coded[n].astype(jnp.int32).astype(jnp.float32) * landed_steps[n]
        grad = lax.dot_general(
            both[:, KA:],
            both[:, :KA],
            (((0,), (0,)), ((), ())),
            precision=lax.Precision.HIGHEST,
            preferred_element_type=jnp.float32,
        )
        ratios.append((grad / scale).reshape(SLICES, DEPTH, KA))
    rows[...] = jnp.concatenate(ratios, axis=1).astype(jnp.bfloat16)

    def row_copy(k):
        return pltpu.make_async_remote_copy(
            src_ref=rows.at[k],
            dst_ref=gathered.at[spot],
            send_sem=row_send.at[k],
            recv_sem=row_recv.at[spot],
            device_id=(home + FIRST + k // 4, k % 4),
            device_id_type=MESH,
        )

    def row_arrival(i):
        return pltpu.make_async_remote_copy(
            src_ref=rows.at[0],
            dst_ref=gathered.at[i],
            send_sem=row_send.at[0],
            recv_sem=row_recv.at[i],
            device_id=(home + i // 4, i % 4),
            device_id_type=MESH,
        )

    def value_copy(i):
        return pltpu.make_async_remote_copy(
            src_ref=scores.at[i],
            dst_ref=returned.at[me],
            send_sem=val_send.at[i],
            recv_sem=val_recv.at[me],
            device_id=(home + i // 4, i % 4),
            device_id_type=MESH,
        )

    def value_arrival(k):
        return pltpu.make_async_remote_copy(
            src_ref=scores.at[0],
            dst_ref=returned.at[k],
            send_sem=val_send.at[0],
            recv_sem=val_recv.at[k],
            device_id=(home + FIRST + k // 4, k % 4),
            device_id_type=MESH,
        )

    def elsewhere(k):
        return (home + FIRST + k // 4 != ex) | (k % 4 != tp)

    turn = jnp.where(place < DISTRICT // 2, SLICES // 2, 0)

    def to_all(step):
        for j in range(SLICES):
            k = (j + turn) % SLICES
            when(elsewhere(k), lambda k=k: step(k))

    to_all(lambda k: row_copy(k).start())

    @pl.when(centre)
    def _():
        gathered[spot] = rows[me]

    for copy in tables:
        copy.wait()
    slot_total = cand_ref.shape[1]
    line = lax.broadcasted_iota(jnp.int32, (examples * slot_total, 1), 0)
    codes = jnp.full((examples * slot_total, 1), -1, jnp.int32)
    for n in range(examples):
        for s in range(slot_total):
            code = jnp.where(s < count_ref[n], map_ref[cand_ref[n, s]], -1)
            codes = jnp.where(line == n * slot_total + s, code, codes)
    load_q.wait()

    @pl.when(centre)
    def _():
        for batch in range(BATCHES):
            held = range(batch * SHARE, (batch + 1) * SHARE)
            for i in held:
                when(i != spot, lambda i=i: row_arrival(i).wait_recv())
            wide[...] = (
                gathered[pl.ds(batch * SHARE, SHARE)]
                .astype(jnp.float32)
                .reshape(SHARE * examples * DEPTH, KA)
            )
            lines = jnp.concatenate(
                [wide[pl.ds(g, SHARE * examples, stride=DEPTH), :] for g in range(DEPTH)], axis=1
            ).astype(jnp.bfloat16)
            if batch == 0:
                others(each, lambda e: take_query(e).wait_recv())
            values = lax.dot_general(
                lines,
                query_v[...],
                (((1,), (1,)), ((), ())),
                preferred_element_type=jnp.float32,
            )
            for at, i in enumerate(held):
                scores[i] = values[at * examples : (at + 1) * examples, :]
            for i in held:
                when(i != spot, lambda i=i: value_copy(i).start())
        returned[me] = scores[spot]

    for copy in (*first, *sum(across, ()), *second):
        copy.wait_send()
    to_all(lambda k: row_copy(k).wait_send())
    others(to_centres, lambda e: pass_query(e).wait_send())
    to_all(lambda k: value_arrival(k).wait_recv())
    sums = jnp.sum(returned[...], axis=0)
    total = sums.shape[1]
    block = lax.broadcasted_iota(jnp.int32, (1, total), 1) // queries
    spread = jnp.concatenate(
        [jnp.broadcast_to(sums[n : n + 1], (slot_total, total)) for n in range(examples)], axis=0
    )
    kept = jnp.where(block == codes, spread, 0.0)
    lanes = sum(kept[:, a : a + 128] for a in range(0, total, 128))
    chosen = sum(lanes[:, a : a + queries] for a in range(0, 128, queries))
    for n in range(examples):
        out_ref[n] = chosen[n * slot_total : (n + 1) * slot_total]

    @pl.when(centre)
    def _():
        for i in range(SOURCES):
            when(i != spot, lambda i=i: value_copy(i).wait_send())


def shards(acts, out_grads, basis_in, basis_out, eigen, query_grads, candidates, counts, owner_map):
    owners = lax.axis_size("ex")
    assert lax.axis_size("tp") == 4 and owners % DISTRICT == 0
    examples, slot_total = candidates.shape
    tokens = examples * SEQ
    queries = query_grads.shape[0]
    width = query_grads.shape[1] // SLICES
    assert query_grads.shape[1] == KA * KG and 128 % queries == 0
    vmem = pltpu.VMEM
    dma = pltpu.SemaphoreType.DMA
    return pl.pallas_call(
        functools.partial(kernel, owners, examples),
        out_shape=jax.ShapeDtypeStruct((examples, slot_total, queries), jnp.float32),
        in_specs=[pl.BlockSpec(memory_space=pl.ANY)] * 9,
        out_specs=pl.BlockSpec(memory_space=pltpu.VMEM),
        scratch_shapes=[
            vmem((4, tokens, acts.shape[1]), jnp.bfloat16),
            vmem((4, tokens, out_grads.shape[1]), jnp.bfloat16),
            vmem(basis_in.shape, jnp.bfloat16),
            vmem(basis_out.shape, jnp.bfloat16),
            vmem(eigen.shape, jnp.float32),
            vmem((owners * queries, width), jnp.bfloat16),
            vmem((TEAM, queries, width), jnp.bfloat16),
            vmem((4, tokens, KA + KG), jnp.float32),
            vmem((2, tokens, KA + KG), jnp.float32),
            vmem((examples, SEQ, KA + KG), jnp.int16),
            vmem((examples, 1, KA + KG), jnp.float32),
            vmem((examples, SEQ, KA + KG), jnp.int16),
            vmem((examples, 1, KA + KG), jnp.float32),
            vmem((SLICES, examples * DEPTH, KA), jnp.bfloat16),
            vmem((SOURCES, examples * DEPTH, KA), jnp.bfloat16),
            vmem((SHARE * examples * DEPTH, KA), jnp.float32),
            vmem((SOURCES, examples, owners * queries), jnp.float32),
            vmem((SLICES, examples, owners * queries), jnp.float32),
            pltpu.SMEM(candidates.shape, jnp.int32),
            pltpu.SMEM(counts.shape, jnp.int32),
            pltpu.SMEM(owner_map.shape, jnp.int32),
            dma((7 + TEAM,)),
            dma((8 * examples,)),
            dma((4 * examples,)),
            dma((4 * examples,)),
            dma((owners,)),
            dma((owners,)),
            dma((SLICES,)),
            dma((SOURCES,)),
            dma((SOURCES,)),
            dma((SLICES,)),
            pltpu.SemaphoreType.REGULAR((2,)),
            pltpu.SemaphoreType.REGULAR((owners,)),
            pltpu.SemaphoreType.REGULAR,
        ],
        compiler_params=pltpu.CompilerParams(
            collective_id=0, has_side_effects=True, vmem_limit_bytes=60 << 20
        ),
    )(acts, out_grads, basis_in, basis_out, eigen, query_grads, candidates, counts, owner_map)


def solution(mesh):
    in_specs = (
        P("ex", "tp"),
        P("ex", "tp"),
        P("tp", None),
        P("tp", None),
        P(),
        P("ex", None),
        P(("ex", "tp"), None),
        P(("ex", "tp")),
        P(),
    )
    out_specs = P(("ex", "tp"), None, None)
    return jax.shard_map(shards, mesh=mesh, in_specs=in_specs, out_specs=out_specs, check_vma=False)
```

```python
import functools

import jax
import jax.numpy as jnp
from jax import lax
from jax.experimental import pallas as pl
from jax.experimental.pallas import tpu as pltpu
from jax.sharding import PartitionSpec as P

MESH = pl.DeviceIdType.MESH
KA = 128
KG = 128
SEQ = 128
DAMP = 0.05
DISTRICT = 8
FIRST = 2
TEAM = 4
SLICES = 4 * TEAM
SOURCES = 4 * DISTRICT
BATCHES = 2
SHARE = SOURCES // BATCHES
DEPTH = KG // SLICES
PAIR = 2
LEVELS = 32767.0
TINY = 1e-30


def each(first, last, step):
    def body(i, carry):
        step(i)
        return carry

    lax.fori_loop(first, last, body, 0)


def kernel(
    owners,
    examples,
    acts_ref,
    grads_ref,
    bin_ref,
    bout_ref,
    eigen_ref,
    query_ref,
    cand_in,
    count_in,
    map_in,
    out_ref,
    acts_v,
    grads_v,
    bin_v,
    bout_v,
    eigen_v,
    query_v,
    staged,
    part_in,
    part_out,
    landed_in,
    landed_out,
    coded_in,
    steps_in,
    coded_out,
    steps_out,
    landed_coded_in,
    landed_steps_in,
    landed_coded_out,
    landed_steps_out,
    rows,
    gathered,
    wide,
    scores,
    returned,
    cand_ref,
    count_ref,
    map_ref,
    load_sem,
    piece_sem,
    tp_send,
    tp_recv,
    query_send,
    query_recv,
    row_send,
    row_recv,
    val_send,
    val_recv,
    tp_ready,
    ready,
    team_ready,
):
    ex = lax.axis_index("ex")
    tp = lax.axis_index("tp")
    place = ex % DISTRICT
    home = ex - place
    spot = place * 4 + tp
    centre = (place >= FIRST) & (place < FIRST + TEAM)
    me = jnp.where(centre, (place - FIRST) * 4 + tp, 0)
    y, c = tp // 2, tp % 2
    near = 2 * y + (1 - c)
    far = 2 * (1 - y) + c
    tokens = examples * SEQ
    queries = query_ref.shape[0]
    width = query_ref.shape[1] // SLICES

    barrier = pltpu.get_barrier_semaphore()

    def greet(sem, e, t):
        pl.semaphore_signal(sem, inc=1, device_id=(e, t), device_id_type=MESH)

    def await_all(sem, count):
        @pl.when(count > 0)
        def _():
            pl.semaphore_wait(sem, count)

    def is_centre(e):
        at = e % DISTRICT
        return (at >= FIRST) & (at < FIRST + TEAM)

    def linked(first, last, step):
        def visit(e):
            pl.when(centre | is_centre(e))(lambda: step(e))

        each(first, last, visit)

    def number(first, last):
        def count(e, sofar):
            return sofar + (centre | is_centre(e)).astype(jnp.int32)

        return lax.fori_loop(first, last, count, 0)

    def when(condition, step):
        @pl.when(condition)
        def _():
            step()

    when(c == 0, lambda: greet(barrier, ex, near))
    when(y == 0, lambda: greet(barrier, ex, far))

    chunks = (2 * (1 - y) + (1 - c), far, near, tp)

    def load(src, dst, sem):
        return pltpu.make_async_copy(src, dst, load_sem.at[sem])

    load_b = (load(bin_ref, bin_v, 0), load(bout_ref, bout_v, 1))
    load_e = load(eigen_ref, eigen_v, 2)
    own_rows = pl.ds(pl.multiple_of(ex * queries, queries), queries)

    def slice_of(l):
        return query_ref.at[:, pl.ds(pl.multiple_of((l * 4 + tp) * width, width), width)]

    load_q = load(slice_of(jnp.where(centre, place - FIRST, 0)), query_v.at[own_rows], 3)
    load_s = [load(slice_of(l), staged.at[l], 7 + l) for l in range(TEAM)]
    tables = (
        load(cand_in, cand_ref, 4),
        load(count_in, count_ref, 5),
        load(map_in, map_ref, 6),
    )
    pieces = {}
    for i, d in enumerate(chunks):
        at = i * (1 + examples)
        rows_of = pl.ds(pl.multiple_of(d * tokens, tokens), tokens)
        pieces[i, "in"] = pltpu.make_async_copy(
            acts_ref.at[rows_of], acts_v.at[i], piece_sem.at[at]
        )
        for n in range(examples):
            here = pl.ds(pl.multiple_of(d * tokens + n * SEQ, SEQ), SEQ)
            pieces[i, n] = pltpu.make_async_copy(
                grads_ref.at[here], grads_v.at[i, pl.ds(n * SEQ, SEQ)], piece_sem.at[at + 1 + n]
            )
    sequences = range(examples)

    def fetch(*copies):
        for copy in copies:
            copy.start()

    fetch(*load_s, load_b[0], pieces[0, "in"], pieces[1, "in"])
    fetch(load_b[1], pieces[0, 0], pieces[1, 0])

    linked(ex + 1, owners, lambda e: greet(barrier, e, tp))
    await_all(barrier, c + y + number(0, ex))
    when(c == 1, lambda: greet(tp_ready.at[0], ex, near))
    when(y == 1, lambda: greet(tp_ready.at[1], ex, far))
    when(centre, lambda: each(0, ex, lambda e: greet(ready.at[ex], e, tp)))

    def pass_query(e):
        return pltpu.make_async_remote_copy(
            src_ref=staged.at[e % DISTRICT - FIRST],
            dst_ref=query_v.at[own_rows],
            send_sem=query_send.at[e],
            recv_sem=query_recv.at[ex],
            device_id=(e, tp),
            device_id_type=MESH,
        )

    def take_query(e):
        return pltpu.make_async_remote_copy(
            src_ref=staged.at[0],
            dst_ref=query_v.at[pl.ds(pl.multiple_of(e * queries, queries), queries)],
            send_sem=query_send.at[e],
            recv_sem=query_recv.at[e],
            device_id=(e, tp),
            device_id_type=MESH,
        )

    def to_centres(first, last, step):
        def visit(e):
            pl.when(is_centre(e))(lambda: step(e))

        each(first, last, visit)

    def others(visit, step):
        visit(0, ex, step)
        visit(ex + 1, owners, step)


    def project_in(i):
        pieces[i, "in"].wait()
        part_in[i] = jnp.dot(acts_v[i], bin_v[...], preferred_element_type=jnp.float32)

    def project_out(i, n):
        pieces[i, n].wait()
        span = pl.ds(n * SEQ, SEQ)
        part_out[i, span] = jnp.dot(
            grads_v[i, span], bout_v[...], preferred_element_type=jnp.float32
        )

    sent = []

    def send(src, dst, peer):
        sem = len(sent)
        copy = pltpu.make_async_remote_copy(
            src_ref=src,
            dst_ref=dst,
            send_sem=tp_send.at[sem],
            recv_sem=tp_recv.at[sem],
            device_id=(ex, peer),
            device_id_type=MESH,
        )
        copy.start()
        sent.append(copy)
        return copy

    def near_in(i, slot):
        return send(part_in.at[i], landed_in.at[slot], near)

    def near_out(i, slot, n):
        span = pl.ds(n * SEQ, SEQ)
        return send(part_out.at[i, span], landed_out.at[slot, span], near)

    def encode(both, coded, steps, n):
        top = jnp.maximum(jnp.max(jnp.abs(both), axis=0, keepdims=True), TINY)
        steps[n] = top * (1.0 / LEVELS)
        coded[n] = jnp.round(both * (LEVELS / top)).astype(jnp.int32).astype(jnp.int16)

    def forward_in():
        first_in.wait_recv()
        for n in sequences:
            span = slice(n * SEQ, (n + 1) * SEQ)
            encode(part_in[1, span] + landed_in[0, span], coded_in, steps_in, n)
        when(y == 0, lambda: pl.semaphore_wait(tp_ready.at[1], 1))
        return send(coded_in, landed_coded_in, far), send(steps_in, landed_steps_in, far)

    def forward_out(n):
        first_out[n].wait_recv()
        span = slice(n * SEQ, (n + 1) * SEQ)
        encode(part_out[1, span] + landed_out[0, span], coded_out, steps_out, n)
        return (
            send(coded_out.at[n], landed_coded_out.at[n], far),
            send(steps_out.at[n], landed_steps_out.at[n], far),
        )

    def pass_up(e):
        pl.semaphore_wait(ready.at[e], 1)
        pass_query(e).start()

    soon = jnp.minimum((ex // PAIR + 2) * PAIR, owners)
    for copy in load_s:
        copy.wait()
    to_centres(0, ex, lambda e: pass_query(e).start())
    load_b[0].wait()
    project_in(0)
    when(c == 0, lambda: pl.semaphore_wait(tp_ready.at[0], 1))
    first_in, first_out, across_out = near_in(0, 0), [], []
    for n in sequences[1:]:
        fetch(pieces[0, n], pieces[1, n])
    project_in(1)
    to_centres(ex + 1, soon, pass_up)
    load_b[1].wait()
    for n in sequences:
        project_out(0, n)
        first_out.append(near_out(0, 0, n))
        if n == 0:
            across_in = forward_in()
        else:
            across_out.append(forward_out(n - 1))
        if n == examples - 1:
            to_centres(soon, owners, pass_up)
        project_out(1, n)
    across_out.append(forward_out(examples - 1))
    fetch(*(pieces[i, part] for i in (2, 3) for part in ("in", *sequences)), load_e, load_q, *tables)
    project_in(2)
    second_in, second_out = near_in(2, 1), []
    for n in sequences:
        project_out(2, n)
        second_out.append(near_out(2, 1, n))
    project_in(3)
    for n in sequences:
        project_out(3, n)
    load_e.wait()
    scale = (eigen_v[...] + DAMP) * SEQ

    def split(value):
        high = value.astype(jnp.bfloat16)
        return high, (value - high.astype(jnp.float32)).astype(jnp.bfloat16)

    def decode(coded, steps, n):
        return coded[n].astype(jnp.int32).astype(jnp.float32) * steps[n]

    second_in.wait_recv()
    for copy in across_in:
        copy.wait_recv()
    when(centre, lambda: each(home, ex, lambda e: greet(team_ready, e, tp)))
    ratios = []
    for n in sequences:
        span = slice(n * SEQ, (n + 1) * SEQ)
        second_out[n].wait_recv()
        pin = part_in[3, span] + landed_in[1, span]
        pout = part_out[3, span] + landed_out[1, span]
        for copy in across_out[n]:
            copy.wait_recv()
        pin_high, pin_low = split(pin + decode(landed_coded_in, landed_steps_in, n))
        pout_high, pout_low = split(pout + decode(landed_coded_out, landed_steps_out, n))
        grad = lax.dot_general(
            jnp.concatenate([pout_high, pout_high, pout_low], axis=0),
            jnp.concatenate([pin_high, pin_low, pin_high], axis=0),
            (((0,), (0,)), ((), ())),
            preferred_element_type=jnp.float32,
        )
        ratios.append((grad / scale).reshape(SLICES, DEPTH, KA))
    rows[...] = jnp.concatenate(ratios, axis=1).astype(jnp.bfloat16)

    def row_copy(k):
        return pltpu.make_async_remote_copy(
            src_ref=rows.at[k],
            dst_ref=gathered.at[spot],
            send_sem=row_send.at[k],
            recv_sem=row_recv.at[spot],
            device_id=(home + FIRST + k // 4, k % 4),
            device_id_type=MESH,
        )

    def row_arrival(i):
        return pltpu.make_async_remote_copy(
            src_ref=rows.at[0],
            dst_ref=gathered.at[i],
            send_sem=row_send.at[0],
            recv_sem=row_recv.at[i],
            device_id=(home + i // 4, i % 4),
            device_id_type=MESH,
        )

    def value_copy(i):
        return pltpu.make_async_remote_copy(
            src_ref=scores.at[i],
            dst_ref=returned.at[me],
            send_sem=val_send.at[i],
            recv_sem=val_recv.at[me],
            device_id=(home + i // 4, i % 4),
            device_id_type=MESH,
        )

    def value_arrival(k):
        return pltpu.make_async_remote_copy(
            src_ref=scores.at[0],
            dst_ref=returned.at[k],
            send_sem=val_send.at[0],
            recv_sem=val_recv.at[k],
            device_id=(home + FIRST + k // 4, k % 4),
            device_id_type=MESH,
        )

    def elsewhere(k):
        return (home + FIRST + k // 4 != ex) | (k % 4 != tp)

    turn = jnp.where(place < DISTRICT // 2, SLICES // 2, 0)

    def to_all(step):
        for j in range(SLICES):
            k = (j + turn) % SLICES
            when(elsewhere(k), lambda k=k: step(k))

    above = jnp.maximum(place + 1, FIRST)
    await_all(team_ready, jnp.maximum(FIRST + TEAM - above, 0))
    to_all(lambda k: row_copy(k).start())

    @pl.when(centre)
    def _():
        gathered[spot] = rows[me]

    for copy in tables:
        copy.wait()
    slot_total = cand_ref.shape[1]
    line = lax.broadcasted_iota(jnp.int32, (examples * slot_total, 1), 0)
    codes = jnp.full((examples * slot_total, 1), -1, jnp.int32)
    for n in range(examples):
        for s in range(slot_total):
            code = jnp.where(s < count_ref[n], map_ref[cand_ref[n, s]], -1)
            codes = jnp.where(line == n * slot_total + s, code, codes)
    load_q.wait()

    @pl.when(centre)
    def _():
        for batch in range(BATCHES):
            held = range(batch * SHARE, (batch + 1) * SHARE)
            for i in held:
                when(i != spot, lambda i=i: row_arrival(i).wait_recv())
            wide[...] = (
                gathered[pl.ds(batch * SHARE, SHARE)]
                .astype(jnp.float32)
                .reshape(SHARE * examples * DEPTH, KA)
            )
            lines = jnp.concatenate(
                [wide[pl.ds(g, SHARE * examples, stride=DEPTH), :] for g in range(DEPTH)], axis=1
            ).astype(jnp.bfloat16)
            if batch == 0:
                others(each, lambda e: take_query(e).wait_recv())
            values = lax.dot_general(
                lines,
                query_v[...],
                (((1,), (1,)), ((), ())),
                preferred_element_type=jnp.float32,
            )
            for at, i in enumerate(held):
                scores[i] = values[at * examples : (at + 1) * examples, :]
            for i in held:
                when(i != spot, lambda i=i: value_copy(i).start())
        returned[me] = scores[spot]

    for copy in sent:
        copy.wait_send()
    to_all(lambda k: row_copy(k).wait_send())
    others(to_centres, lambda e: pass_query(e).wait_send())
    to_all(lambda k: value_arrival(k).wait_recv())
    sums = jnp.sum(returned[...], axis=0)
    total = sums.shape[1]
    block = lax.broadcasted_iota(jnp.int32, (1, total), 1) // queries
    spread = jnp.concatenate(
        [jnp.broadcast_to(sums[n : n + 1], (slot_total, total)) for n in range(examples)], axis=0
    )
    kept = jnp.where(block == codes, spread, 0.0)
    lanes = sum(kept[:, a : a + 128] for a in range(0, total, 128))
    chosen = sum(lanes[:, a : a + queries] for a in range(0, 128, queries))
    for n in range(examples):
        out_ref[n] = chosen[n * slot_total : (n + 1) * slot_total]

    @pl.when(centre)
    def _():
        for i in range(SOURCES):
            when(i != spot, lambda i=i: value_copy(i).wait_send())


def shards(acts, out_grads, basis_in, basis_out, eigen, query_grads, candidates, counts, owner_map):
    owners = lax.axis_size("ex")
    assert lax.axis_size("tp") == 4 and owners % DISTRICT == 0
    examples, slot_total = candidates.shape
    tokens = examples * SEQ
    queries = query_grads.shape[0]
    width = query_grads.shape[1] // SLICES
    assert query_grads.shape[1] == KA * KG and 128 % queries == 0
    vmem = pltpu.VMEM
    dma = pltpu.SemaphoreType.DMA
    return pl.pallas_call(
        functools.partial(kernel, owners, examples),
        out_shape=jax.ShapeDtypeStruct((examples, slot_total, queries), jnp.float32),
        in_specs=[pl.BlockSpec(memory_space=pl.ANY)] * 9,
        out_specs=pl.BlockSpec(memory_space=pltpu.VMEM),
        scratch_shapes=[
            vmem((4, tokens, acts.shape[1]), jnp.bfloat16),
            vmem((4, tokens, out_grads.shape[1]), jnp.bfloat16),
            vmem(basis_in.shape, jnp.bfloat16),
            vmem(basis_out.shape, jnp.bfloat16),
            vmem(eigen.shape, jnp.float32),
            vmem((owners * queries, width), jnp.bfloat16),
            vmem((TEAM, queries, width), jnp.bfloat16),
            vmem((4, tokens, KA), jnp.float32),
            vmem((4, tokens, KG), jnp.float32),
            vmem((2, tokens, KA), jnp.float32),
            vmem((2, tokens, KG), jnp.float32),
            vmem((examples, SEQ, KA), jnp.int16),
            vmem((examples, 1, KA), jnp.float32),
            vmem((examples, SEQ, KG), jnp.int16),
            vmem((examples, 1, KG), jnp.float32),
            vmem((examples, SEQ, KA), jnp.int16),
            vmem((examples, 1, KA), jnp.float32),
            vmem((examples, SEQ, KG), jnp.int16),
            vmem((examples, 1, KG), jnp.float32),
            vmem((SLICES, examples * DEPTH, KA), jnp.bfloat16),
            vmem((SOURCES, examples * DEPTH, KA), jnp.bfloat16),
            vmem((SHARE * examples * DEPTH, KA), jnp.float32),
            vmem((SOURCES, examples, owners * queries), jnp.float32),
            vmem((SLICES, examples, owners * queries), jnp.float32),
            pltpu.SMEM(candidates.shape, jnp.int32),
            pltpu.SMEM(counts.shape, jnp.int32),
            pltpu.SMEM(owner_map.shape, jnp.int32),
            dma((7 + TEAM,)),
            dma((4 + 4 * examples,)),
            dma((4 + 4 * examples,)),
            dma((4 + 4 * examples,)),
            dma((owners,)),
            dma((owners,)),
            dma((SLICES,)),
            dma((SOURCES,)),
            dma((SOURCES,)),
            dma((SLICES,)),
            pltpu.SemaphoreType.REGULAR((2,)),
            pltpu.SemaphoreType.REGULAR((owners,)),
            pltpu.SemaphoreType.REGULAR,
        ],
        compiler_params=pltpu.CompilerParams(
            collective_id=0, has_side_effects=True, vmem_limit_bytes=60 << 20
        ),
    )(acts, out_grads, basis_in, basis_out, eigen, query_grads, candidates, counts, owner_map)


def solution(mesh):
    in_specs = (
        P("ex", "tp"),
        P("ex", "tp"),
        P("tp", None),
        P("tp", None),
        P(),
        P("ex", None),
        P(("ex", "tp"), None),
        P(("ex", "tp")),
        P(),
    )
    out_specs = P(("ex", "tp"), None, None)
    return jax.shard_map(shards, mesh=mesh, in_specs=in_specs, out_specs=out_specs, check_vma=False)
```

```python
import functools

import jax
import jax.numpy as jnp
from jax import lax
from jax.experimental import pallas as pl
from jax.experimental.pallas import tpu as pltpu
from jax.sharding import PartitionSpec as P

MESH = pl.DeviceIdType.MESH
KA = 128
KG = 128
SEQ = 128
DAMP = 0.05
DISTRICT = 8
FIRST = 2
TEAM = 4
SLICES = 4 * TEAM
SOURCES = 4 * DISTRICT
BATCHES = 2
SHARE = SOURCES // BATCHES
DEPTH = KG // SLICES
PAIR = 2
LEVELS = 32767.0
TINY = 1e-30


def each(first, last, step):
    def body(i, carry):
        step(i)
        return carry

    lax.fori_loop(first, last, body, 0)


def kernel(
    owners,
    examples,
    acts_ref,
    grads_ref,
    bin_ref,
    bout_ref,
    eigen_ref,
    query_ref,
    cand_in,
    count_in,
    map_in,
    out_ref,
    acts_v,
    grads_v,
    bin_v,
    bout_v,
    eigen_v,
    query_v,
    staged,
    part_in,
    part_out,
    landed_in,
    landed_out,
    coded_in,
    steps_in,
    coded_out,
    steps_out,
    landed_coded_in,
    landed_steps_in,
    landed_coded_out,
    landed_steps_out,
    rows,
    gathered,
    wide,
    scores,
    returned,
    cand_ref,
    count_ref,
    map_ref,
    load_sem,
    piece_sem,
    tp_send,
    tp_recv,
    query_send,
    query_recv,
    row_send,
    row_recv,
    val_send,
    val_recv,
    tp_ready,
    ready,
    team_ready,
):
    ex = lax.axis_index("ex")
    tp = lax.axis_index("tp")
    place = ex % DISTRICT
    home = ex - place
    spot = place * 4 + tp
    centre = (place >= FIRST) & (place < FIRST + TEAM)
    me = jnp.where(centre, (place - FIRST) * 4 + tp, 0)
    y, c = tp // 2, tp % 2
    near = 2 * y + (1 - c)
    far = 2 * (1 - y) + c
    cross = 2 * (1 - y) + (1 - c)
    tokens = examples * SEQ
    queries = query_ref.shape[0]
    width = query_ref.shape[1] // SLICES

    barrier = pltpu.get_barrier_semaphore()

    def greet(sem, e, t):
        pl.semaphore_signal(sem, inc=1, device_id=(e, t), device_id_type=MESH)

    def await_all(sem, count):
        @pl.when(count > 0)
        def _():
            pl.semaphore_wait(sem, count)

    def is_centre(e):
        at = e % DISTRICT
        return (at >= FIRST) & (at < FIRST + TEAM)

    def linked(first, last, step):
        def visit(e):
            pl.when(centre | is_centre(e))(lambda: step(e))

        each(first, last, visit)

    def number(first, last):
        def count(e, sofar):
            return sofar + (centre | is_centre(e)).astype(jnp.int32)

        return lax.fori_loop(first, last, count, 0)

    def when(condition, step):
        @pl.when(condition)
        def _():
            step()

    when(c == 0, lambda: greet(barrier, ex, near))
    when(y == 0, lambda: greet(barrier, ex, far))
    when(y == 0, lambda: greet(barrier, ex, cross))

    chunks = (cross, far, near, tp)

    def load(src, dst, sem):
        return pltpu.make_async_copy(src, dst, load_sem.at[sem])

    load_b = (load(bin_ref, bin_v, 0), load(bout_ref, bout_v, 1))
    load_e = load(eigen_ref, eigen_v, 2)
    own_rows = pl.ds(pl.multiple_of(ex * queries, queries), queries)

    def slice_of(l):
        return query_ref.at[:, pl.ds(pl.multiple_of((l * 4 + tp) * width, width), width)]

    load_q = load(slice_of(jnp.where(centre, place - FIRST, 0)), query_v.at[own_rows], 3)
    load_s = [load(slice_of(l), staged.at[l], 7 + l) for l in range(TEAM)]
    tables = (
        load(cand_in, cand_ref, 4),
        load(count_in, count_ref, 5),
        load(map_in, map_ref, 6),
    )
    pieces = {}
    for i, d in enumerate(chunks):
        at = i * (1 + examples)
        rows_of = pl.ds(pl.multiple_of(d * tokens, tokens), tokens)
        pieces[i, "in"] = pltpu.make_async_copy(
            acts_ref.at[rows_of], acts_v.at[i], piece_sem.at[at]
        )
        for n in range(examples):
            here = pl.ds(pl.multiple_of(d * tokens + n * SEQ, SEQ), SEQ)
            pieces[i, n] = pltpu.make_async_copy(
                grads_ref.at[here], grads_v.at[i, pl.ds(n * SEQ, SEQ)], piece_sem.at[at + 1 + n]
            )
    sequences = range(examples)

    def fetch(*copies):
        for copy in copies:
            copy.start()

    fetch(*load_s, load_b[0], pieces[0, "in"], pieces[1, "in"])
    fetch(load_b[1], pieces[0, 0], pieces[1, 0])

    linked(ex + 1, owners, lambda e: greet(barrier, e, tp))
    await_all(barrier, c + 2 * y + number(0, ex))
    when(c == 1, lambda: greet(tp_ready.at[0], ex, near))
    when(y == 1, lambda: greet(tp_ready.at[1], ex, far))
    when(y == 1, lambda: greet(tp_ready.at[2], ex, cross))
    when(centre, lambda: each(0, ex, lambda e: greet(ready.at[ex], e, tp)))

    def pass_query(e):
        return pltpu.make_async_remote_copy(
            src_ref=staged.at[e % DISTRICT - FIRST],
            dst_ref=query_v.at[own_rows],
            send_sem=query_send.at[e],
            recv_sem=query_recv.at[ex],
            device_id=(e, tp),
            device_id_type=MESH,
        )

    def take_query(e):
        return pltpu.make_async_remote_copy(
            src_ref=staged.at[0],
            dst_ref=query_v.at[pl.ds(pl.multiple_of(e * queries, queries), queries)],
            send_sem=query_send.at[e],
            recv_sem=query_recv.at[e],
            device_id=(e, tp),
            device_id_type=MESH,
        )

    def to_centres(first, last, step):
        def visit(e):
            pl.when(is_centre(e))(lambda: step(e))

        each(first, last, visit)

    def others(visit, step):
        visit(0, ex, step)
        visit(ex + 1, owners, step)


    def project_in(i):
        pieces[i, "in"].wait()
        part_in[i] = jnp.dot(acts_v[i], bin_v[...], preferred_element_type=jnp.float32)

    def project_out(i, n):
        pieces[i, n].wait()
        span = pl.ds(n * SEQ, SEQ)
        part_out[i, span] = jnp.dot(
            grads_v[i, span], bout_v[...], preferred_element_type=jnp.float32
        )

    sent = []

    def send(src, dst, peer):
        sem = len(sent)
        copy = pltpu.make_async_remote_copy(
            src_ref=src,
            dst_ref=dst,
            send_sem=tp_send.at[sem],
            recv_sem=tp_recv.at[sem],
            device_id=(ex, peer),
            device_id_type=MESH,
        )
        copy.start()
        sent.append(copy)
        return copy

    def near_in(i, slot):
        return send(part_in.at[i], landed_in.at[slot], near)

    def near_out(i, slot, n):
        span = pl.ds(n * SEQ, SEQ)
        return send(part_out.at[i, span], landed_out.at[slot, span], near)

    def encode(both, coded, steps, n):
        top = jnp.maximum(jnp.max(jnp.abs(both), axis=0, keepdims=True), TINY)
        steps[n] = top * (1.0 / LEVELS)
        coded[n] = jnp.round(both * (LEVELS / top)).astype(jnp.int32).astype(jnp.int16)

    def forward_in():
        first_in.wait_recv()
        for n in sequences:
            span = slice(n * SEQ, (n + 1) * SEQ)
            encode(part_in[1, span] + landed_in[0, span], coded_in, steps_in, n)
        when(y == 0, lambda: pl.semaphore_wait(tp_ready.at[1], 1))
        return send(coded_in, landed_coded_in, far), send(steps_in, landed_steps_in, far)

    def forward_out(n):
        first_out[n].wait_recv()
        span = slice(n * SEQ, (n + 1) * SEQ)
        encode(part_out[1, span] + landed_out[0, span], coded_out, steps_out, n)
        return (
            send(coded_out.at[n], landed_coded_out.at[n], far),
            send(steps_out.at[n], landed_steps_out.at[n], far),
        )

    def pass_up(e):
        pl.semaphore_wait(ready.at[e], 1)
        pass_query(e).start()

    soon = jnp.minimum((ex // PAIR + 2) * PAIR, owners)
    for copy in load_s:
        copy.wait()
    to_centres(0, ex, lambda e: pass_query(e).start())
    load_b[0].wait()
    project_in(0)
    when(c == 0, lambda: pl.semaphore_wait(tp_ready.at[0], 1))
    first_in, first_out, across_out = near_in(0, 0), [], []
    for n in sequences[1:]:
        fetch(pieces[0, n], pieces[1, n])
    project_in(1)
    to_centres(ex + 1, soon, pass_up)
    load_b[1].wait()
    for n in sequences:
        project_out(0, n)
        first_out.append(near_out(0, 0, n))
        if n == 0:
            across_in = forward_in()
        else:
            across_out.append(forward_out(n - 1))
        if n == examples - 1:
            to_centres(soon, owners, pass_up)
        project_out(1, n)
    across_out.append(forward_out(examples - 1))
    when(y == 0, lambda: pl.semaphore_wait(tp_ready.at[2], 1))
    when(centre, lambda: each(home, ex, lambda e: greet(team_ready, e, tp)))
    fetch(*(pieces[i, part] for i in (2, 3) for part in ("in", *sequences)), load_e, load_q, *tables)
    project_in(2)
    second_in, second_out = near_in(2, 1), []
    for n in sequences:
        project_out(2, n)
        second_out.append(near_out(2, 1, n))
    project_in(3)
    for n in sequences:
        project_out(3, n)
    load_e.wait()
    scale = (eigen_v[...] + DAMP) * SEQ

    def split(value):
        high = value.astype(jnp.bfloat16)
        return high, (value - high.astype(jnp.float32)).astype(jnp.bfloat16)

    def decode(coded, steps, n):
        return coded[n].astype(jnp.int32).astype(jnp.float32) * steps[n]

    second_in.wait_recv()
    for copy in across_in:
        copy.wait_recv()
    ratios = []
    for n in sequences:
        span = slice(n * SEQ, (n + 1) * SEQ)
        second_out[n].wait_recv()
        pin = part_in[3, span] + landed_in[1, span]
        pout = part_out[3, span] + landed_out[1, span]
        for copy in across_out[n]:
            copy.wait_recv()
        pin_high, pin_low = split(pin + decode(landed_coded_in, landed_steps_in, n))
        pout_high, pout_low = split(pout + decode(landed_coded_out, landed_steps_out, n))
        grad = lax.dot_general(
            jnp.concatenate([pout_high, pout_high, pout_low], axis=0),
            jnp.concatenate([pin_high, pin_low, pin_high], axis=0),
            (((0,), (0,)), ((), ())),
            preferred_element_type=jnp.float32,
        )
        ratios.append((grad / scale).reshape(SLICES, DEPTH, KA))
    rows[...] = jnp.concatenate(ratios, axis=1).astype(jnp.bfloat16)

    def row_copy(k):
        return pltpu.make_async_remote_copy(
            src_ref=rows.at[k],
            dst_ref=gathered.at[spot],
            send_sem=row_send.at[k],
            recv_sem=row_recv.at[spot],
            device_id=(home + FIRST + k // 4, k % 4),
            device_id_type=MESH,
        )

    def row_arrival(i):
        return pltpu.make_async_remote_copy(
            src_ref=rows.at[0],
            dst_ref=gathered.at[i],
            send_sem=row_send.at[0],
            recv_sem=row_recv.at[i],
            device_id=(home + i // 4, i % 4),
            device_id_type=MESH,
        )

    def value_copy(i):
        return pltpu.make_async_remote_copy(
            src_ref=scores.at[i],
            dst_ref=returned.at[me],
            send_sem=val_send.at[i],
            recv_sem=val_recv.at[me],
            device_id=(home + i // 4, i % 4),
            device_id_type=MESH,
        )

    def value_arrival(k):
        return pltpu.make_async_remote_copy(
            src_ref=scores.at[0],
            dst_ref=returned.at[k],
            send_sem=val_send.at[0],
            recv_sem=val_recv.at[k],
            device_id=(home + FIRST + k // 4, k % 4),
            device_id_type=MESH,
        )

    def elsewhere(k):
        return (home + FIRST + k // 4 != ex) | (k % 4 != tp)

    turn = jnp.where(place < DISTRICT // 2, SLICES // 2, 0)

    def to_all(step):
        for j in range(SLICES):
            k = (j + turn) % SLICES
            when(elsewhere(k), lambda k=k: step(k))

    above = jnp.maximum(place + 1, FIRST)
    await_all(team_ready, jnp.maximum(FIRST + TEAM - above, 0))
    to_all(lambda k: row_copy(k).start())

    @pl.when(centre)
    def _():
        gathered[spot] = rows[me]

    for copy in tables:
        copy.wait()
    slot_total = cand_ref.shape[1]
    line = lax.broadcasted_iota(jnp.int32, (examples * slot_total, 1), 0)
    codes = jnp.full((examples * slot_total, 1), -1, jnp.int32)
    for n in range(examples):
        for s in range(slot_total):
            code = jnp.where(s < count_ref[n], map_ref[cand_ref[n, s]], -1)
            codes = jnp.where(line == n * slot_total + s, code, codes)
    load_q.wait()

    @pl.when(centre)
    def _():
        for batch in range(BATCHES):
            held = range(batch * SHARE, (batch + 1) * SHARE)
            for i in held:
                when(i != spot, lambda i=i: row_arrival(i).wait_recv())
            wide[...] = (
                gathered[pl.ds(batch * SHARE, SHARE)]
                .astype(jnp.float32)
                .reshape(SHARE * examples * DEPTH, KA)
            )
            lines = jnp.concatenate(
                [wide[pl.ds(g, SHARE * examples, stride=DEPTH), :] for g in range(DEPTH)], axis=1
            ).astype(jnp.bfloat16)
            if batch == 0:
                others(each, lambda e: take_query(e).wait_recv())
            values = lax.dot_general(
                lines,
                query_v[...],
                (((1,), (1,)), ((), ())),
                preferred_element_type=jnp.float32,
            )
            for at, i in enumerate(held):
                scores[i] = values[at * examples : (at + 1) * examples, :]
            for i in held:
                when(i != spot, lambda i=i: value_copy(i).start())
        returned[me] = scores[spot]

    for copy in sent:
        copy.wait_send()
    to_all(lambda k: row_copy(k).wait_send())
    others(to_centres, lambda e: pass_query(e).wait_send())
    to_all(lambda k: value_arrival(k).wait_recv())
    sums = jnp.sum(returned[...], axis=0)
    total = sums.shape[1]
    block = lax.broadcasted_iota(jnp.int32, (1, total), 1) // queries
    spread = jnp.concatenate(
        [jnp.broadcast_to(sums[n : n + 1], (slot_total, total)) for n in range(examples)], axis=0
    )
    kept = jnp.where(block == codes, spread, 0.0)
    lanes = sum(kept[:, a : a + 128] for a in range(0, total, 128))
    chosen = sum(lanes[:, a : a + queries] for a in range(0, 128, queries))
    for n in range(examples):
        out_ref[n] = chosen[n * slot_total : (n + 1) * slot_total]

    @pl.when(centre)
    def _():
        for i in range(SOURCES):
            when(i != spot, lambda i=i: value_copy(i).wait_send())


def shards(acts, out_grads, basis_in, basis_out, eigen, query_grads, candidates, counts, owner_map):
    owners = lax.axis_size("ex")
    assert lax.axis_size("tp") == 4 and owners % DISTRICT == 0
    examples, slot_total = candidates.shape
    tokens = examples * SEQ
    queries = query_grads.shape[0]
    width = query_grads.shape[1] // SLICES
    assert query_grads.shape[1] == KA * KG and 128 % queries == 0
    vmem = pltpu.VMEM
    dma = pltpu.SemaphoreType.DMA
    return pl.pallas_call(
        functools.partial(kernel, owners, examples),
        out_shape=jax.ShapeDtypeStruct((examples, slot_total, queries), jnp.float32),
        in_specs=[pl.BlockSpec(memory_space=pl.ANY)] * 9,
        out_specs=pl.BlockSpec(memory_space=pltpu.VMEM),
        scratch_shapes=[
            vmem((4, tokens, acts.shape[1]), jnp.bfloat16),
            vmem((4, tokens, out_grads.shape[1]), jnp.bfloat16),
            vmem(basis_in.shape, jnp.bfloat16),
            vmem(basis_out.shape, jnp.bfloat16),
            vmem(eigen.shape, jnp.float32),
            vmem((owners * queries, width), jnp.bfloat16),
            vmem((TEAM, queries, width), jnp.bfloat16),
            vmem((4, tokens, KA), jnp.float32),
            vmem((4, tokens, KG), jnp.float32),
            vmem((2, tokens, KA), jnp.float32),
            vmem((2, tokens, KG), jnp.float32),
            vmem((examples, SEQ, KA), jnp.int16),
            vmem((examples, 1, KA), jnp.float32),
            vmem((examples, SEQ, KG), jnp.int16),
            vmem((examples, 1, KG), jnp.float32),
            vmem((examples, SEQ, KA), jnp.int16),
            vmem((examples, 1, KA), jnp.float32),
            vmem((examples, SEQ, KG), jnp.int16),
            vmem((examples, 1, KG), jnp.float32),
            vmem((SLICES, examples * DEPTH, KA), jnp.bfloat16),
            vmem((SOURCES, examples * DEPTH, KA), jnp.bfloat16),
            vmem((SHARE * examples * DEPTH, KA), jnp.float32),
            vmem((SOURCES, examples, owners * queries), jnp.float32),
            vmem((SLICES, examples, owners * queries), jnp.float32),
            pltpu.SMEM(candidates.shape, jnp.int32),
            pltpu.SMEM(counts.shape, jnp.int32),
            pltpu.SMEM(owner_map.shape, jnp.int32),
            dma((7 + TEAM,)),
            dma((4 + 4 * examples,)),
            dma((4 + 4 * examples,)),
            dma((4 + 4 * examples,)),
            dma((owners,)),
            dma((owners,)),
            dma((SLICES,)),
            dma((SOURCES,)),
            dma((SOURCES,)),
            dma((SLICES,)),
            pltpu.SemaphoreType.REGULAR((3,)),
            pltpu.SemaphoreType.REGULAR((owners,)),
            pltpu.SemaphoreType.REGULAR,
        ],
        compiler_params=pltpu.CompilerParams(
            collective_id=0, has_side_effects=True, vmem_limit_bytes=60 << 20
        ),
    )(acts, out_grads, basis_in, basis_out, eigen, query_grads, candidates, counts, owner_map)


def solution(mesh):
    in_specs = (
        P("ex", "tp"),
        P("ex", "tp"),
        P("tp", None),
        P("tp", None),
        P(),
        P("ex", None),
        P(("ex", "tp"), None),
        P(("ex", "tp")),
        P(),
    )
    out_specs = P(("ex", "tp"), None, None)
    return jax.shard_map(shards, mesh=mesh, in_specs=in_specs, out_specs=out_specs, check_vma=False)
```

```python
import functools

import jax
import jax.numpy as jnp
from jax import lax
from jax.experimental import pallas as pl
from jax.experimental.pallas import tpu as pltpu
from jax.sharding import PartitionSpec as P

MESH = pl.DeviceIdType.MESH
KA = 128
KG = 128
SEQ = 128
DAMP = 0.05
DISTRICT = 8
FIRST = 2
TEAM = 4
SLICES = 4 * TEAM
SOURCES = 4 * DISTRICT
BATCHES = 2
SHARE = SOURCES // BATCHES
DEPTH = KG // SLICES
PAIR = 2
LEVELS = 32767.0
TINY = 1e-30


def each(first, last, step):
    def body(i, carry):
        step(i)
        return carry

    lax.fori_loop(first, last, body, 0)


def kernel(
    owners,
    examples,
    acts_ref,
    grads_ref,
    bin_ref,
    bout_ref,
    eigen_ref,
    query_ref,
    cand_in,
    count_in,
    map_in,
    out_ref,
    acts_v,
    grads_v,
    bin_v,
    bout_v,
    eigen_v,
    query_v,
    staged,
    part_in,
    part_out,
    landed_in,
    landed_out,
    coded_in,
    steps_in,
    coded_out,
    steps_out,
    landed_coded_in,
    landed_steps_in,
    landed_coded_out,
    landed_steps_out,
    rows,
    gathered,
    wide,
    scores,
    returned,
    cand_ref,
    count_ref,
    map_ref,
    load_sem,
    piece_sem,
    tp_send,
    tp_recv,
    query_send,
    query_recv,
    row_send,
    row_recv,
    val_send,
    val_recv,
    tp_ready,
    ready,
    team_ready,
):
    ex = lax.axis_index("ex")
    tp = lax.axis_index("tp")
    place = ex % DISTRICT
    home = ex - place
    spot = place * 4 + tp
    centre = (place >= FIRST) & (place < FIRST + TEAM)
    me = jnp.where(centre, (place - FIRST) * 4 + tp, 0)
    y, c = tp // 2, tp % 2
    near = 2 * y + (1 - c)
    far = 2 * (1 - y) + c
    cross = 2 * (1 - y) + (1 - c)
    tokens = examples * SEQ
    queries = query_ref.shape[0]
    width = query_ref.shape[1] // SLICES

    barrier = pltpu.get_barrier_semaphore()

    def greet(sem, e, t):
        pl.semaphore_signal(sem, inc=1, device_id=(e, t), device_id_type=MESH)

    def await_all(sem, count):
        @pl.when(count > 0)
        def _():
            pl.semaphore_wait(sem, count)

    def is_centre(e):
        at = e % DISTRICT
        return (at >= FIRST) & (at < FIRST + TEAM)

    def linked(first, last, step):
        def visit(e):
            pl.when(centre | is_centre(e))(lambda: step(e))

        each(first, last, visit)

    def number(first, last):
        def count(e, sofar):
            return sofar + (centre | is_centre(e)).astype(jnp.int32)

        return lax.fori_loop(first, last, count, 0)

    def when(condition, step):
        @pl.when(condition)
        def _():
            step()

    when(c == 0, lambda: greet(barrier, ex, near))
    when(y == 0, lambda: greet(barrier, ex, far))
    when(y == 0, lambda: greet(barrier, ex, cross))

    chunks = (cross, far, near, tp)

    def load(src, dst, sem):
        return pltpu.make_async_copy(src, dst, load_sem.at[sem])

    load_b = (load(bin_ref, bin_v, 0), load(bout_ref, bout_v, 1))
    load_e = load(eigen_ref, eigen_v, 2)
    own_rows = pl.ds(pl.multiple_of(ex * queries, queries), queries)

    def slice_of(l):
        return query_ref.at[:, pl.ds(pl.multiple_of((l * 4 + tp) * width, width), width)]

    load_q = load(slice_of(jnp.where(centre, place - FIRST, 0)), query_v.at[own_rows], 3)
    load_s = [load(slice_of(l), staged.at[l], 7 + l) for l in range(TEAM)]
    tables = (
        load(cand_in, cand_ref, 4),
        load(count_in, count_ref, 5),
        load(map_in, map_ref, 6),
    )
    pieces = {}
    for i, d in enumerate(chunks):
        at = i * (1 + examples)
        rows_of = pl.ds(pl.multiple_of(d * tokens, tokens), tokens)
        pieces[i, "in"] = pltpu.make_async_copy(
            acts_ref.at[rows_of], acts_v.at[i], piece_sem.at[at]
        )
        for n in range(examples):
            here = pl.ds(pl.multiple_of(d * tokens + n * SEQ, SEQ), SEQ)
            pieces[i, n] = pltpu.make_async_copy(
                grads_ref.at[here], grads_v.at[i, pl.ds(n * SEQ, SEQ)], piece_sem.at[at + 1 + n]
            )
    sequences = range(examples)

    def fetch(*copies):
        for copy in copies:
            copy.start()

    fetch(*load_s, load_b[0], pieces[0, "in"], pieces[1, "in"])
    fetch(load_b[1], pieces[0, 0], pieces[1, 0])

    linked(ex + 1, owners, lambda e: greet(barrier, e, tp))
    await_all(barrier, c + 2 * y + number(0, ex))
    when(c == 1, lambda: greet(tp_ready.at[0], ex, near))
    when(y == 1, lambda: greet(tp_ready.at[1], ex, far))
    when(y == 1, lambda: greet(tp_ready.at[2], ex, cross))
    when(centre, lambda: each(0, ex, lambda e: greet(ready.at[ex], e, tp)))

    def pass_query(e):
        return pltpu.make_async_remote_copy(
            src_ref=staged.at[e % DISTRICT - FIRST],
            dst_ref=query_v.at[own_rows],
            send_sem=query_send.at[e],
            recv_sem=query_recv.at[ex],
            device_id=(e, tp),
            device_id_type=MESH,
        )

    def take_query(e):
        return pltpu.make_async_remote_copy(
            src_ref=staged.at[0],
            dst_ref=query_v.at[pl.ds(pl.multiple_of(e * queries, queries), queries)],
            send_sem=query_send.at[e],
            recv_sem=query_recv.at[e],
            device_id=(e, tp),
            device_id_type=MESH,
        )

    def to_centres(first, last, step):
        def visit(e):
            pl.when(is_centre(e))(lambda: step(e))

        each(first, last, visit)

    def others(visit, step):
        visit(0, ex, step)
        visit(ex + 1, owners, step)


    def project_in(i):
        pieces[i, "in"].wait()
        part_in[i] = jnp.dot(acts_v[i], bin_v[...], preferred_element_type=jnp.float32)

    def project_out(i, n):
        pieces[i, n].wait()
        span = pl.ds(n * SEQ, SEQ)
        part_out[i, span] = jnp.dot(
            grads_v[i, span], bout_v[...], preferred_element_type=jnp.float32
        )

    sent = []

    def send(src, dst, peer):
        sem = len(sent)
        copy = pltpu.make_async_remote_copy(
            src_ref=src,
            dst_ref=dst,
            send_sem=tp_send.at[sem],
            recv_sem=tp_recv.at[sem],
            device_id=(ex, peer),
            device_id_type=MESH,
        )
        copy.start()
        sent.append(copy)
        return copy

    def near_in(i, slot):
        return send(part_in.at[i], landed_in.at[slot], near)

    def near_out(i, slot, n):
        span = pl.ds(n * SEQ, SEQ)
        return send(part_out.at[i, span], landed_out.at[slot, span], near)

    def encode(both, coded, steps, n):
        top = jnp.maximum(jnp.max(jnp.abs(both), axis=0, keepdims=True), TINY)
        steps[n] = top * (1.0 / LEVELS)
        coded[n] = jnp.round(both * (LEVELS / top)).astype(jnp.int32).astype(jnp.int16)

    def forward_in():
        first_in.wait_recv()
        for n in sequences:
            span = slice(n * SEQ, (n + 1) * SEQ)
            encode(part_in[1, span] + landed_in[0, span], coded_in, steps_in, n)
        when(y == 0, lambda: pl.semaphore_wait(tp_ready.at[1], 1))
        return send(coded_in, landed_coded_in, far), send(steps_in, landed_steps_in, far)

    def forward_out(n):
        first_out[n].wait_recv()
        span = slice(n * SEQ, (n + 1) * SEQ)
        encode(part_out[1, span] + landed_out[0, span], coded_out, steps_out, n)
        return (
            send(coded_out.at[n], landed_coded_out.at[n], far),
            send(steps_out.at[n], landed_steps_out.at[n], far),
        )

    def pass_up(e):
        pl.semaphore_wait(ready.at[e], 1)
        pass_query(e).start()

    soon = jnp.minimum((ex // PAIR + 2) * PAIR, owners)
    for copy in load_s:
        copy.wait()
    to_centres(0, ex, lambda e: pass_query(e).start())
    load_b[0].wait()
    project_in(0)
    when(c == 0, lambda: pl.semaphore_wait(tp_ready.at[0], 1))
    first_in, first_out, across_out = near_in(0, 0), [], []
    for n in sequences[1:]:
        fetch(pieces[0, n], pieces[1, n])
    project_in(1)
    to_centres(ex + 1, soon, pass_up)
    load_b[1].wait()
    for n in sequences:
        project_out(0, n)
        first_out.append(near_out(0, 0, n))
        if n == 0:
            fetch(*(pieces[2, part] for part in ("in", *sequences)))
        if n == examples - 1:
            fetch(*(pieces[3, part] for part in ("in", *sequences)))
        if n == 0:
            across_in = forward_in()
        else:
            across_out.append(forward_out(n - 1))
        if n == examples - 1:
            to_centres(soon, owners, pass_up)
        project_out(1, n)
    across_out.append(forward_out(examples - 1))
    when(y == 0, lambda: pl.semaphore_wait(tp_ready.at[2], 1))
    when(centre, lambda: each(home, ex, lambda e: greet(team_ready, e, tp)))
    fetch(load_e, load_q, *tables)
    project_in(2)
    second_in, second_out = near_in(2, 1), []
    for n in sequences:
        project_out(2, n)
        second_out.append(near_out(2, 1, n))
    project_in(3)
    for n in sequences:
        project_out(3, n)
    load_e.wait()
    scale = (eigen_v[...] + DAMP) * SEQ

    def split(value):
        high = value.astype(jnp.bfloat16)
        return high, (value - high.astype(jnp.float32)).astype(jnp.bfloat16)

    def decode(coded, steps, n):
        return coded[n].astype(jnp.int32).astype(jnp.float32) * steps[n]

    second_in.wait_recv()
    for copy in across_in:
        copy.wait_recv()
    ratios = []
    for n in sequences:
        span = slice(n * SEQ, (n + 1) * SEQ)
        second_out[n].wait_recv()
        pin = part_in[3, span] + landed_in[1, span]
        pout = part_out[3, span] + landed_out[1, span]
        for copy in across_out[n]:
            copy.wait_recv()
        pin_high, pin_low = split(pin + decode(landed_coded_in, landed_steps_in, n))
        pout_high, pout_low = split(pout + decode(landed_coded_out, landed_steps_out, n))
        grad = lax.dot_general(
            jnp.concatenate([pout_high, pout_high, pout_low], axis=0),
            jnp.concatenate([pin_high, pin_low, pin_high], axis=0),
            (((0,), (0,)), ((), ())),
            preferred_element_type=jnp.float32,
        )
        ratios.append((grad / scale).reshape(SLICES, DEPTH, KA))
    rows[...] = jnp.concatenate(ratios, axis=1).astype(jnp.bfloat16)

    def row_copy(k):
        return pltpu.make_async_remote_copy(
            src_ref=rows.at[k],
            dst_ref=gathered.at[spot],
            send_sem=row_send.at[k],
            recv_sem=row_recv.at[spot],
            device_id=(home + FIRST + k // 4, k % 4),
            device_id_type=MESH,
        )

    def row_arrival(i):
        return pltpu.make_async_remote_copy(
            src_ref=rows.at[0],
            dst_ref=gathered.at[i],
            send_sem=row_send.at[0],
            recv_sem=row_recv.at[i],
            device_id=(home + i // 4, i % 4),
            device_id_type=MESH,
        )

    def value_copy(i):
        return pltpu.make_async_remote_copy(
            src_ref=scores.at[i],
            dst_ref=returned.at[me],
            send_sem=val_send.at[i],
            recv_sem=val_recv.at[me],
            device_id=(home + i // 4, i % 4),
            device_id_type=MESH,
        )

    def value_arrival(k):
        return pltpu.make_async_remote_copy(
            src_ref=scores.at[0],
            dst_ref=returned.at[k],
            send_sem=val_send.at[0],
            recv_sem=val_recv.at[k],
            device_id=(home + FIRST + k // 4, k % 4),
            device_id_type=MESH,
        )

    def elsewhere(k):
        return (home + FIRST + k // 4 != ex) | (k % 4 != tp)

    turn = jnp.where(place < DISTRICT // 2, SLICES // 2, 0)

    def to_all(step):
        for j in range(SLICES):
            k = (j + turn) % SLICES
            when(elsewhere(k), lambda k=k: step(k))

    above = jnp.maximum(place + 1, FIRST)
    await_all(team_ready, jnp.maximum(FIRST + TEAM - above, 0))
    to_all(lambda k: row_copy(k).start())

    @pl.when(centre)
    def _():
        gathered[spot] = rows[me]

    for copy in tables:
        copy.wait()
    slot_total = cand_ref.shape[1]
    line = lax.broadcasted_iota(jnp.int32, (examples * slot_total, 1), 0)
    codes = jnp.full((examples * slot_total, 1), -1, jnp.int32)
    for n in range(examples):
        for s in range(slot_total):
            code = jnp.where(s < count_ref[n], map_ref[cand_ref[n, s]], -1)
            codes = jnp.where(line == n * slot_total + s, code, codes)
    load_q.wait()

    @pl.when(centre)
    def _():
        for batch in range(BATCHES):
            held = range(batch * SHARE, (batch + 1) * SHARE)
            for i in held:
                when(i != spot, lambda i=i: row_arrival(i).wait_recv())
            wide[...] = (
                gathered[pl.ds(batch * SHARE, SHARE)]
                .astype(jnp.float32)
                .reshape(SHARE * examples * DEPTH, KA)
            )
            lines = jnp.concatenate(
                [wide[pl.ds(g, SHARE * examples, stride=DEPTH), :] for g in range(DEPTH)], axis=1
            ).astype(jnp.bfloat16)
            if batch == 0:
                others(each, lambda e: take_query(e).wait_recv())
            values = lax.dot_general(
                lines,
                query_v[...],
                (((1,), (1,)), ((), ())),
                preferred_element_type=jnp.float32,
            )
            for at, i in enumerate(held):
                scores[i] = values[at * examples : (at + 1) * examples, :]
            for i in held:
                when(i != spot, lambda i=i: value_copy(i).start())
        returned[me] = scores[spot]

    for copy in sent:
        copy.wait_send()
    to_all(lambda k: row_copy(k).wait_send())
    others(to_centres, lambda e: pass_query(e).wait_send())
    to_all(lambda k: value_arrival(k).wait_recv())
    sums = jnp.sum(returned[...], axis=0)
    total = sums.shape[1]
    block = lax.broadcasted_iota(jnp.int32, (1, total), 1) // queries
    spread = jnp.concatenate(
        [jnp.broadcast_to(sums[n : n + 1], (slot_total, total)) for n in range(examples)], axis=0
    )
    kept = jnp.where(block == codes, spread, 0.0)
    lanes = sum(kept[:, a : a + 128] for a in range(0, total, 128))
    chosen = sum(lanes[:, a : a + queries] for a in range(0, 128, queries))
    for n in range(examples):
        out_ref[n] = chosen[n * slot_total : (n + 1) * slot_total]

    @pl.when(centre)
    def _():
        for i in range(SOURCES):
            when(i != spot, lambda i=i: value_copy(i).wait_send())


def shards(acts, out_grads, basis_in, basis_out, eigen, query_grads, candidates, counts, owner_map):
    owners = lax.axis_size("ex")
    assert lax.axis_size("tp") == 4 and owners % DISTRICT == 0
    examples, slot_total = candidates.shape
    tokens = examples * SEQ
    queries = query_grads.shape[0]
    width = query_grads.shape[1] // SLICES
    assert query_grads.shape[1] == KA * KG and 128 % queries == 0
    vmem = pltpu.VMEM
    dma = pltpu.SemaphoreType.DMA
    return pl.pallas_call(
        functools.partial(kernel, owners, examples),
        out_shape=jax.ShapeDtypeStruct((examples, slot_total, queries), jnp.float32),
        in_specs=[pl.BlockSpec(memory_space=pl.ANY)] * 9,
        out_specs=pl.BlockSpec(memory_space=pltpu.VMEM),
        scratch_shapes=[
            vmem((4, tokens, acts.shape[1]), jnp.bfloat16),
            vmem((4, tokens, out_grads.shape[1]), jnp.bfloat16),
            vmem(basis_in.shape, jnp.bfloat16),
            vmem(basis_out.shape, jnp.bfloat16),
            vmem(eigen.shape, jnp.float32),
            vmem((owners * queries, width), jnp.bfloat16),
            vmem((TEAM, queries, width), jnp.bfloat16),
            vmem((4, tokens, KA), jnp.float32),
            vmem((4, tokens, KG), jnp.float32),
            vmem((2, tokens, KA), jnp.float32),
            vmem((2, tokens, KG), jnp.float32),
            vmem((examples, SEQ, KA), jnp.int16),
            vmem((examples, 1, KA), jnp.float32),
            vmem((examples, SEQ, KG), jnp.int16),
            vmem((examples, 1, KG), jnp.float32),
            vmem((examples, SEQ, KA), jnp.int16),
            vmem((examples, 1, KA), jnp.float32),
            vmem((examples, SEQ, KG), jnp.int16),
            vmem((examples, 1, KG), jnp.float32),
            vmem((SLICES, examples * DEPTH, KA), jnp.bfloat16),
            vmem((SOURCES, examples * DEPTH, KA), jnp.bfloat16),
            vmem((SHARE * examples * DEPTH, KA), jnp.float32),
            vmem((SOURCES, examples, owners * queries), jnp.float32),
            vmem((SLICES, examples, owners * queries), jnp.float32),
            pltpu.SMEM(candidates.shape, jnp.int32),
            pltpu.SMEM(counts.shape, jnp.int32),
            pltpu.SMEM(owner_map.shape, jnp.int32),
            dma((7 + TEAM,)),
            dma((4 + 4 * examples,)),
            dma((4 + 4 * examples,)),
            dma((4 + 4 * examples,)),
            dma((owners,)),
            dma((owners,)),
            dma((SLICES,)),
            dma((SOURCES,)),
            dma((SOURCES,)),
            dma((SLICES,)),
            pltpu.SemaphoreType.REGULAR((3,)),
            pltpu.SemaphoreType.REGULAR((owners,)),
            pltpu.SemaphoreType.REGULAR,
        ],
        compiler_params=pltpu.CompilerParams(
            collective_id=0, has_side_effects=True, vmem_limit_bytes=60 << 20
        ),
    )(acts, out_grads, basis_in, basis_out, eigen, query_grads, candidates, counts, owner_map)


def solution(mesh):
    in_specs = (
        P("ex", "tp"),
        P("ex", "tp"),
        P("tp", None),
        P("tp", None),
        P(),
        P("ex", None),
        P(("ex", "tp"), None),
        P(("ex", "tp")),
        P(),
    )
    out_specs = P(("ex", "tp"), None, None)
    return jax.shard_map(shards, mesh=mesh, in_specs=in_specs, out_specs=out_specs, check_vma=False)
```

```python
import functools

import jax
import jax.numpy as jnp
from jax import lax
from jax.experimental import pallas as pl
from jax.experimental.pallas import tpu as pltpu
from jax.sharding import PartitionSpec as P

MESH = pl.DeviceIdType.MESH
KA = 128
KG = 128
SEQ = 128
DAMP = 0.05
DISTRICT = 8
FIRST = 2
TEAM = 4
SLICES = 4 * TEAM
SOURCES = 4 * DISTRICT
BATCHES = 2
SHARE = SOURCES // BATCHES
DEPTH = KG // SLICES
PAIR = 2
LEVELS = 32767.0
TINY = 1e-30


def each(first, last, step):
    def body(i, carry):
        step(i)
        return carry

    lax.fori_loop(first, last, body, 0)


def kernel(
    owners,
    examples,
    acts_ref,
    grads_ref,
    bin_ref,
    bout_ref,
    eigen_ref,
    query_ref,
    cand_in,
    count_in,
    map_in,
    out_ref,
    acts_v,
    grads_v,
    bin_v,
    bout_v,
    eigen_v,
    query_v,
    staged,
    part_in,
    part_out,
    landed_in,
    landed_out,
    coded_in,
    steps_in,
    coded_out,
    steps_out,
    landed_coded_in,
    landed_steps_in,
    landed_coded_out,
    landed_steps_out,
    rows,
    gathered,
    wide,
    scores,
    returned,
    cand_ref,
    count_ref,
    map_ref,
    load_sem,
    piece_sem,
    tp_send,
    tp_recv,
    query_send,
    query_recv,
    row_send,
    row_recv,
    val_send,
    val_recv,
    tp_ready,
    ready,
    team_ready,
):
    ex = lax.axis_index("ex")
    tp = lax.axis_index("tp")
    place = ex % DISTRICT
    home = ex - place
    spot = place * 4 + tp
    centre = (place >= FIRST) & (place < FIRST + TEAM)
    me = jnp.where(centre, (place - FIRST) * 4 + tp, 0)
    y, c = tp // 2, tp % 2
    near = 2 * y + (1 - c)
    far = 2 * (1 - y) + c
    cross = 2 * (1 - y) + (1 - c)
    tokens = examples * SEQ
    queries = query_ref.shape[0]
    width = query_ref.shape[1] // SLICES

    barrier = pltpu.get_barrier_semaphore()

    def greet(sem, e, t):
        pl.semaphore_signal(sem, inc=1, device_id=(e, t), device_id_type=MESH)

    def await_all(sem, count):
        @pl.when(count > 0)
        def _():
            pl.semaphore_wait(sem, count)

    def is_centre(e):
        at = e % DISTRICT
        return (at >= FIRST) & (at < FIRST + TEAM)

    def to_centres(first, last, step):
        def visit(e):
            pl.when(is_centre(e))(lambda: step(e))

        each(first, last, visit)

    def when(condition, step):
        @pl.when(condition)
        def _():
            step()

    when(c == 0, lambda: greet(barrier, ex, near))
    when(y == 0, lambda: greet(barrier, ex, far))
    when(y == 0, lambda: greet(barrier, ex, cross))

    chunks = (cross, far, near, tp)

    def load(src, dst, sem):
        return pltpu.make_async_copy(src, dst, load_sem.at[sem])

    load_b = (load(bin_ref, bin_v, 0), load(bout_ref, bout_v, 1))
    load_e = load(eigen_ref, eigen_v, 2)
    own_rows = pl.ds(pl.multiple_of(ex * queries, queries), queries)

    def slice_of(l):
        return query_ref.at[:, pl.ds(pl.multiple_of((l * 4 + tp) * width, width), width)]

    load_q = pltpu.make_async_copy(
        slice_of(jnp.where(centre, place - FIRST, 0)), query_v.at[own_rows], query_recv.at[0]
    )
    load_s = [load(slice_of(l), staged.at[l], 7 + l) for l in range(TEAM)]
    tables = (
        load(cand_in, cand_ref, 4),
        load(count_in, count_ref, 5),
        load(map_in, map_ref, 6),
    )
    pieces = {}
    for i, d in enumerate(chunks):
        at = i * (1 + examples)
        rows_of = pl.ds(pl.multiple_of(d * tokens, tokens), tokens)
        pieces[i, "in"] = pltpu.make_async_copy(
            acts_ref.at[rows_of], acts_v.at[i], piece_sem.at[at]
        )
        for n in range(examples):
            here = pl.ds(pl.multiple_of(d * tokens + n * SEQ, SEQ), SEQ)
            pieces[i, n] = pltpu.make_async_copy(
                grads_ref.at[here], grads_v.at[i, pl.ds(n * SEQ, SEQ)], piece_sem.at[at + 1 + n]
            )
    sequences = range(examples)

    def fetch(*copies):
        for copy in copies:
            copy.start()

    fetch(load_b[0], pieces[0, "in"], pieces[1, "in"], *load_s)
    fetch(load_b[1], pieces[0, 0], pieces[1, 0])

    @pl.when(centre)
    def _():
        each(ex + 1, owners, lambda e: greet(barrier, e, tp))

    @pl.when(jnp.logical_not(centre))
    def _():
        to_centres(ex + 1, owners, lambda e: greet(barrier, e, tp))

    passed = home // DISTRICT * TEAM + jnp.clip(place - FIRST, 0, TEAM)
    await_all(barrier, c + 2 * y + jnp.where(centre, ex, passed))
    when(c == 1, lambda: greet(tp_ready.at[0], ex, near))
    when(y == 1, lambda: greet(tp_ready.at[1], ex, far))
    when(y == 1, lambda: greet(tp_ready.at[2], ex, cross))
    when(centre, lambda: each(0, ex, lambda e: greet(ready.at[ex], e, tp)))

    def pass_query(e):
        return pltpu.make_async_remote_copy(
            src_ref=staged.at[e % DISTRICT - FIRST],
            dst_ref=query_v.at[own_rows],
            send_sem=query_send.at[e],
            recv_sem=query_recv.at[0],
            device_id=(e, tp),
            device_id_type=MESH,
        )

    def others(visit, step):
        visit(0, ex, step)
        visit(ex + 1, owners, step)


    def project_in(i):
        pieces[i, "in"].wait()
        part_in[i] = jnp.dot(acts_v[i], bin_v[...], preferred_element_type=jnp.float32)

    def project_out(i, n):
        pieces[i, n].wait()
        span = pl.ds(n * SEQ, SEQ)
        part_out[i, span] = jnp.dot(
            grads_v[i, span], bout_v[...], preferred_element_type=jnp.float32
        )

    sent = []

    def send(src, dst, peer):
        sem = len(sent)
        copy = pltpu.make_async_remote_copy(
            src_ref=src,
            dst_ref=dst,
            send_sem=tp_send.at[sem],
            recv_sem=tp_recv.at[sem],
            device_id=(ex, peer),
            device_id_type=MESH,
        )
        copy.start()
        sent.append(copy)
        return copy

    def near_in(i, slot):
        return send(part_in.at[i], landed_in.at[slot], near)

    def near_out(i, slot, n):
        span = pl.ds(n * SEQ, SEQ)
        return send(part_out.at[i, span], landed_out.at[slot, span], near)

    def encode(both, coded, steps, n):
        top = jnp.maximum(jnp.max(jnp.abs(both), axis=0, keepdims=True), TINY)
        steps[n] = top * (1.0 / LEVELS)
        coded[n] = jnp.round(both * (LEVELS / top)).astype(jnp.int32).astype(jnp.int16)

    def forward_in():
        first_in.wait_recv()
        for n in sequences:
            span = slice(n * SEQ, (n + 1) * SEQ)
            encode(part_in[1, span] + landed_in[0, span], coded_in, steps_in, n)
        when(y == 0, lambda: pl.semaphore_wait(tp_ready.at[1], 1))
        return send(coded_in, landed_coded_in, far), send(steps_in, landed_steps_in, far)

    def forward_out(n):
        first_out[n].wait_recv()
        span = slice(n * SEQ, (n + 1) * SEQ)
        encode(part_out[1, span] + landed_out[0, span], coded_out, steps_out, n)
        return (
            send(coded_out.at[n], landed_coded_out.at[n], far),
            send(steps_out.at[n], landed_steps_out.at[n], far),
        )

    def pass_up(e):
        pl.semaphore_wait(ready.at[e], 1)
        pass_query(e).start()

    soon = jnp.minimum((ex // PAIR + 2) * PAIR, owners)
    load_b[0].wait()
    project_in(0)
    when(c == 0, lambda: pl.semaphore_wait(tp_ready.at[0], 1))
    first_in, first_out, across_out = near_in(0, 0), [], []
    for n in sequences[1:]:
        fetch(pieces[0, n], pieces[1, n])
    project_in(1)
    for copy in load_s:
        copy.wait()
    to_centres(0, ex, lambda e: pass_query(e).start())
    to_centres(ex + 1, soon, pass_up)
    load_b[1].wait()
    for n in sequences:
        project_out(0, n)
        first_out.append(near_out(0, 0, n))
        if n == 0:
            fetch(*(pieces[2, part] for part in ("in", *sequences)))
        if n == examples - 1:
            fetch(*(pieces[3, part] for part in ("in", *sequences)))
        if n == 0:
            across_in = forward_in()
        else:
            across_out.append(forward_out(n - 1))
        if n == examples - 1:
            to_centres(soon, owners, pass_up)
        project_out(1, n)
    across_out.append(forward_out(examples - 1))
    when(y == 0, lambda: pl.semaphore_wait(tp_ready.at[2], 1))
    when(centre, lambda: each(home, ex, lambda e: greet(team_ready, e, tp)))
    fetch(load_e, *tables)
    when(centre, load_q.start)
    project_in(2)
    second_in, second_out = near_in(2, 1), []
    for n in sequences:
        project_out(2, n)
        second_out.append(near_out(2, 1, n))
    project_in(3)
    for n in sequences:
        project_out(3, n)
    load_e.wait()
    scale = (eigen_v[...] + DAMP) * SEQ

    def split(value):
        high = value.astype(jnp.bfloat16)
        return high, (value - high.astype(jnp.float32)).astype(jnp.bfloat16)

    def decode(coded, steps, n):
        return coded[n].astype(jnp.int32).astype(jnp.float32) * steps[n]

    second_in.wait_recv()
    for copy in across_in:
        copy.wait_recv()
    ratios = []
    for n in sequences:
        span = slice(n * SEQ, (n + 1) * SEQ)
        second_out[n].wait_recv()
        pin = part_in[3, span] + landed_in[1, span]
        pout = part_out[3, span] + landed_out[1, span]
        for copy in across_out[n]:
            copy.wait_recv()
        pin_high, pin_low = split(pin + decode(landed_coded_in, landed_steps_in, n))
        pout_high, pout_low = split(pout + decode(landed_coded_out, landed_steps_out, n))
        grad = lax.dot_general(
            jnp.concatenate([pout_high, pout_high, pout_low], axis=0),
            jnp.concatenate([pin_high, pin_low, pin_high], axis=0),
            (((0,), (0,)), ((), ())),
            preferred_element_type=jnp.float32,
        )
        ratios.append((grad / scale).reshape(SLICES, DEPTH, KA))
    rows[...] = jnp.concatenate(ratios, axis=1).astype(jnp.bfloat16)

    def row_copy(k):
        return pltpu.make_async_remote_copy(
            src_ref=rows.at[k],
            dst_ref=gathered.at[spot],
            send_sem=row_send.at[k],
            recv_sem=row_recv.at[spot // SHARE],
            device_id=(home + FIRST + k // 4, k % 4),
            device_id_type=MESH,
        )

    def row_arrivals(batch):
        held = gathered.at[pl.ds(batch * SHARE, SHARE)]
        return pltpu.make_async_copy(held, held, row_recv.at[batch])

    def value_copy(i):
        return pltpu.make_async_remote_copy(
            src_ref=scores.at[i],
            dst_ref=returned.at[me],
            send_sem=val_send.at[i],
            recv_sem=val_recv.at[0],
            device_id=(home + i // 4, i % 4),
            device_id_type=MESH,
        )

    def elsewhere(k):
        return (home + FIRST + k // 4 != ex) | (k % 4 != tp)

    turn = jnp.where(place < DISTRICT // 2, SLICES // 2, 0)

    def to_all(step):
        for j in range(SLICES):
            k = (j + turn) % SLICES
            when(elsewhere(k), lambda k=k: step(k))

    above = jnp.maximum(place + 1, FIRST)
    await_all(team_ready, jnp.maximum(FIRST + TEAM - above, 0))
    to_all(lambda k: row_copy(k).start())

    @pl.when(centre)
    def _():
        pltpu.make_async_copy(
            rows.at[me], gathered.at[spot], row_recv.at[spot // SHARE]
        ).start()

    for copy in tables:
        copy.wait()
    slot_total = cand_ref.shape[1]
    line = lax.broadcasted_iota(jnp.int32, (examples * slot_total, 1), 0)
    codes = jnp.full((examples * slot_total, 1), -1, jnp.int32)
    for n in range(examples):
        for s in range(slot_total):
            code = jnp.where(s < count_ref[n], map_ref[cand_ref[n, s]], -1)
            codes = jnp.where(line == n * slot_total + s, code, codes)

    @pl.when(centre)
    def _():
        for batch in range(BATCHES):
            held = range(batch * SHARE, (batch + 1) * SHARE)
            row_arrivals(batch).wait()
            wide[...] = (
                gathered[pl.ds(batch * SHARE, SHARE)]
                .astype(jnp.float32)
                .reshape(SHARE * examples * DEPTH, KA)
            )
            lines = jnp.concatenate(
                [wide[pl.ds(g, SHARE * examples, stride=DEPTH), :] for g in range(DEPTH)], axis=1
            ).astype(jnp.bfloat16)
            if batch == 0:
                pltpu.make_async_copy(query_v, query_v, query_recv.at[0]).wait()
            values = lax.dot_general(
                lines,
                query_v[...],
                (((1,), (1,)), ((), ())),
                preferred_element_type=jnp.float32,
            )
            for at, i in enumerate(held):
                scores[i] = values[at * examples : (at + 1) * examples, :]
            for i in held:
                when(i != spot, lambda i=i: value_copy(i).start())
            if batch == BATCHES - 1:
                pltpu.make_async_copy(scores.at[spot], returned.at[me], val_recv.at[0]).start()

    for copy in sent:
        copy.wait_send()
    to_all(lambda k: row_copy(k).wait_send())
    others(to_centres, lambda e: pass_query(e).wait_send())
    pltpu.make_async_copy(returned, returned, val_recv.at[0]).wait()
    sums = jnp.sum(returned[...], axis=0)
    total = sums.shape[1]
    block = lax.broadcasted_iota(jnp.int32, (1, total), 1) // queries
    spread = jnp.concatenate(
        [jnp.broadcast_to(sums[n : n + 1], (slot_total, total)) for n in range(examples)], axis=0
    )
    kept = jnp.where(block == codes, spread, 0.0)
    lanes = sum(kept[:, a : a + 128] for a in range(0, total, 128))
    chosen = sum(lanes[:, a : a + queries] for a in range(0, 128, queries))
    for n in range(examples):
        out_ref[n] = chosen[n * slot_total : (n + 1) * slot_total]

    @pl.when(centre)
    def _():
        for i in range(SOURCES):
            when(i != spot, lambda i=i: value_copy(i).wait_send())


def shards(acts, out_grads, basis_in, basis_out, eigen, query_grads, candidates, counts, owner_map):
    owners = lax.axis_size("ex")
    assert lax.axis_size("tp") == 4 and owners % DISTRICT == 0
    examples, slot_total = candidates.shape
    tokens = examples * SEQ
    queries = query_grads.shape[0]
    width = query_grads.shape[1] // SLICES
    assert query_grads.shape[1] == KA * KG and 128 % queries == 0
    vmem = pltpu.VMEM
    dma = pltpu.SemaphoreType.DMA
    return pl.pallas_call(
        functools.partial(kernel, owners, examples),
        out_shape=jax.ShapeDtypeStruct((examples, slot_total, queries), jnp.float32),
        in_specs=[pl.BlockSpec(memory_space=pl.ANY)] * 9,
        out_specs=pl.BlockSpec(memory_space=pltpu.VMEM),
        scratch_shapes=[
            vmem((4, tokens, acts.shape[1]), jnp.bfloat16),
            vmem((4, tokens, out_grads.shape[1]), jnp.bfloat16),
            vmem(basis_in.shape, jnp.bfloat16),
            vmem(basis_out.shape, jnp.bfloat16),
            vmem(eigen.shape, jnp.float32),
            vmem((owners * queries, width), jnp.bfloat16),
            vmem((TEAM, queries, width), jnp.bfloat16),
            vmem((4, tokens, KA), jnp.float32),
            vmem((4, tokens, KG), jnp.float32),
            vmem((2, tokens, KA), jnp.float32),
            vmem((2, tokens, KG), jnp.float32),
            vmem((examples, SEQ, KA), jnp.int16),
            vmem((examples, 1, KA), jnp.float32),
            vmem((examples, SEQ, KG), jnp.int16),
            vmem((examples, 1, KG), jnp.float32),
            vmem((examples, SEQ, KA), jnp.int16),
            vmem((examples, 1, KA), jnp.float32),
            vmem((examples, SEQ, KG), jnp.int16),
            vmem((examples, 1, KG), jnp.float32),
            vmem((SLICES, examples * DEPTH, KA), jnp.bfloat16),
            vmem((SOURCES, examples * DEPTH, KA), jnp.bfloat16),
            vmem((SHARE * examples * DEPTH, KA), jnp.float32),
            vmem((SOURCES, examples, owners * queries), jnp.float32),
            vmem((SLICES, examples, owners * queries), jnp.float32),
            pltpu.SMEM(candidates.shape, jnp.int32),
            pltpu.SMEM(counts.shape, jnp.int32),
            pltpu.SMEM(owner_map.shape, jnp.int32),
            dma((7 + TEAM,)),
            dma((4 + 4 * examples,)),
            dma((4 + 4 * examples,)),
            dma((4 + 4 * examples,)),
            dma((owners,)),
            dma((owners,)),
            dma((SLICES,)),
            dma((SOURCES,)),
            dma((SOURCES,)),
            dma((SLICES,)),
            pltpu.SemaphoreType.REGULAR((3,)),
            pltpu.SemaphoreType.REGULAR((owners,)),
            pltpu.SemaphoreType.REGULAR,
        ],
        compiler_params=pltpu.CompilerParams(
            collective_id=0, has_side_effects=True, vmem_limit_bytes=60 << 20
        ),
    )(acts, out_grads, basis_in, basis_out, eigen, query_grads, candidates, counts, owner_map)


def solution(mesh):
    in_specs = (
        P("ex", "tp"),
        P("ex", "tp"),
        P("tp", None),
        P("tp", None),
        P(),
        P("ex", None),
        P(("ex", "tp"), None),
        P(("ex", "tp")),
        P(),
    )
    out_specs = P(("ex", "tp"), None, None)
    return jax.shard_map(shards, mesh=mesh, in_specs=in_specs, out_specs=out_specs, check_vma=False)
```
